128 devices in a mesh: tm: 4 (over z_hi, core), space: 32 (over x, y, z_lo).
Axes of the slice: x: 4, y: 4, z: 4 (z_hi: 2, z_lo: 2; z = z_hi * 2 + z_lo), core: 2. Of those that a mesh axis runs over, the one named last changes fastest.
Arguments:
- initial: bfloat16 [135, 4096], P(None, 'space'), may hold values from -6 to 6
- forcing: bfloat16 [64, 135, 4096], P('tm', None, 'space'), may hold values from -2 to 2
- damping: float32 [4096], P('space'), may hold values from 0.003 to 0.1
- block_inv: bfloat16 [2, 135, 135], replicated, as said below
- coarse_inv: bfloat16 [2, 135, 135], replicated, as said below
- coupling: bfloat16 [6, 135, 135], replicated, may hold values from -0.078125 to 0.078125
- etype: int32 [32], P('space'), may hold values from 0 to 1
- send_index: int32 [4096], P('space'), may hold values from 0 to 127
- conn: int32 [6, 4096], P(None, 'space'), may hold values from 0 to 255
Outputs:
- states: bfloat16 [64, 135, 4096], P('tm', None, 'space')
The draws below stay inside these ranges and needn't reach their ends.
Inputs may be any that keep to these rules, and one draw needn't show every extreme that they name: block_inv[0] is the inverse of a hexahedron's diagonal block, block_inv[1] that of a prism, with zero rows and columns from 90 on. coarse_inv[0] is the inverse of a hexahedron's coarse diagonal block, coarse_inv[1] that of a prism, with zero rows and columns from 90 on. `send_index`: the first 64 entries of a partition's list name the elements it sends to the partition before, the last 64 those it sends to the partition after. `conn`: entries below 128 name an element of the same partition; the next 64 name the columns received from the partition before, the last 64 those received from the partition after.
All inputs are finite; a program needn't handle non-finite values.
Results may differ from the reference program's by a relative error of at most 0.018.
Values may be sent and summed in bfloat16 or wider, within the bound.
A program may use at most 64 MiB of HBM per device.

```python
import math
import jax
import jax.numpy as jnp
from jax import lax

W = 135
PRISM = 90
FACES = 6
SWEEPS = 2
COARSEN = 4
BLK = 128
E_DEV = 128
HALO = 64
STEPS = 64
ELEMS = 4096
NBLK = 32
SEND = 4096
N_SPACE = 32


def make_inverse(key, shift_value, skew_value):
    inverses = []
    for element_kind in range(2):
        used_rows = W if element_kind == 0 else PRISM
        sub_key = jax.random.fold_in(key, element_kind)
        normals = jax.random.normal(sub_key, (W, W), jnp.float32)
        scales = jax.random.uniform(jax.random.fold_in(sub_key, 7), (W,), jnp.float32, 1.0, 1.1)
        inside = jnp.arange(W) < used_rows
        both_inside = inside[:, None] & inside[None, :]
        skewed = jnp.where(both_inside, (normals - normals.T) / jnp.sqrt(2.0 * W), 0.0)
        matrix = shift_value * jnp.diag(scales) + skew_value * skewed
        inverse = jnp.linalg.solve(matrix, jnp.eye(W, dtype=jnp.float32))
        inverses.append(jnp.where(both_inside, inverse, 0.0))
    return jnp.stack(inverses).astype(jnp.bfloat16)


def draw_block_inv(key, part):
    return make_inverse(jax.random.fold_in(key, 11), 1.03, 0.6)


def draw_coarse_inv(key, part):
    return make_inverse(jax.random.fold_in(key, 23), 1.12, 1.6)


def set_ends(array, stream_key, least, largest):
    longest = array.shape.index(max(array.shape))
    spots = []
    for shift in (0, 1):
        where = [jax.random.randint(jax.random.fold_in(stream_key, axis), (), 0, length) for axis, length in enumerate(array.shape)]
        where[longest] = (where[longest] + shift) % array.shape[longest]
        spots.append(tuple(where))
    return array.at[spots[0]].set(least).at[spots[1]].set(largest)


def level_of(key, dims, shards, low, high):
    level = 1.0
    for position, shards_of in shards:
        heights = jax.random.uniform(jax.random.fold_in(jax.random.fold_in(key, 6), position), (shards_of,), jnp.float32, low / len(shards), high / len(shards))
        level = level * jnp.repeat(jnp.exp(heights), dims[position] // shards_of).reshape((-1,) + (1,) * (len(dims) - 1 - position))
    return level


def scatter_about(key, extent, spread, reach, split=(), kind=jnp.bfloat16):
    result = jax.random.normal(key, extent, jnp.float32) * spread
    if len(split) > 0:
        result = level_of(key, extent, split, -0.22, 0.18) * result
    return jnp.clip(result, min=-reach, max=reach).astype(kind)


def setup_inputs(seed: int = 0) -> dict:
    key_of = jax.random.split(jax.random.key(seed), 10)
    initial = scatter_about(key_of[0], (W, ELEMS), 1.0, 6.0, ((1, 32),))
    forcing = scatter_about(key_of[1], (STEPS, W, ELEMS), 0.3, 2.0, ((0, 4), (2, 32)))
    damping = jnp.clip(jnp.exp(math.log(0.1) - 3.506558 * jax.random.uniform(key_of[2], (ELEMS,), jnp.float32) ** level_of(key_of[2], (ELEMS,), ((0, 32),), -0.2, 0.2)), 0.003, 0.1)
    block_inv = draw_block_inv(jax.random.fold_in(key_of[9], 71), 0)
    coarse_inv = draw_coarse_inv(jax.random.fold_in(key_of[9], 71), 0)
    coupling = scatter_about(key_of[5], (FACES, W, W), (40 * W) ** -0.5, 0.078125)
    etype = set_ends(jax.random.randint(key_of[6], (NBLK,), 0, 2), jax.random.fold_in(key_of[6], 1), 0, 1).astype(jnp.int32)
    send_index = set_ends(jax.random.randint(key_of[7], (SEND,), 0, E_DEV), jax.random.fold_in(key_of[7], 1), 0, E_DEV - 1).astype(jnp.int32)
    conn = set_ends(jax.random.randint(key_of[8], (FACES, ELEMS), 0, E_DEV + 2 * HALO), jax.random.fold_in(key_of[8], 1), 0, (E_DEV + 2 * HALO) - 1).astype(jnp.int32)
    return dict(initial=initial, forcing=forcing, damping=damping, block_inv=block_inv, coarse_inv=coarse_inv, coupling=coupling, etype=etype, send_index=send_index, conn=conn)


def face_tables(etype, conn, send_index):
    element_kinds = jnp.repeat(etype, BLK)
    face_rows = lax.broadcasted_iota(jnp.int32, (FACES, ELEMS), 0)
    keep_faces = ((face_rows < FACES - 1) | (element_kinds[None, :] == 0)).astype(jnp.bfloat16)
    keep_parts = keep_faces.reshape(FACES, N_SPACE, E_DEV).transpose(1, 0, 2)
    conn_parts = conn.reshape(FACES, N_SPACE, E_DEV).transpose(1, 0, 2).reshape(N_SPACE, FACES * E_DEV)
    send_parts = send_index.reshape(N_SPACE, 2 * HALO)
    return (element_kinds, (keep_parts, conn_parts, send_parts))

def coupled_term(iterate, coupling, tables):
    keep_parts, conn_parts, send_parts = tables
    pieces = iterate.reshape(W, N_SPACE, E_DEV)
    outgoing = jnp.take_along_axis(pieces, jnp.broadcast_to(send_parts[None], (W, N_SPACE, 2 * HALO)), axis=2)
    zero_rim = jnp.zeros((W, 1, HALO), jnp.bfloat16)
    from_before = jnp.concatenate([zero_rim, outgoing[:, :-1, HALO:]], axis=1)
    from_after = jnp.concatenate([outgoing[:, 1:, :HALO], zero_rim], axis=1)
    extended = jnp.concatenate([pieces, from_before, from_after], axis=2)
    gathered = jnp.take_along_axis(extended, jnp.broadcast_to(conn_parts[None], (W, N_SPACE, FACES * E_DEV)), axis=2)
    gathered = gathered.reshape(W, N_SPACE, FACES, E_DEV) * keep_parts[None]
    summed = jnp.einsum('fij,jpfk->ipk', coupling.astype(jnp.float32), gathered.astype(jnp.float32))
    return summed.reshape(W, ELEMS)

def apply_inverse(rhs_value, chosen):
    blocked = rhs_value.reshape(W, NBLK, BLK)
    applied = jnp.einsum('bij,jbk->ibk', chosen.astype(jnp.float32), blocked.astype(jnp.float32))
    return applied.reshape(W, ELEMS)

def propagate(start_state, drive_term, chosen, coupling, tables):
    iterate = start_state
    for sweep_index in range(SWEEPS):
        coupled = coupled_term(iterate, coupling, tables)
        rhs_value = (drive_term - coupled).astype(jnp.bfloat16)
        iterate = apply_inverse(rhs_value, chosen).astype(jnp.bfloat16)
    return iterate

def reference(initial, forcing, damping, block_inv, coarse_inv, coupling, etype, send_index, conn):
    element_kinds, tables = face_tables(etype, conn, send_index)
    is_hex = (etype == 0)[:, None, None]
    fine_chosen = jnp.where(is_hex, block_inv[0][None], block_inv[1][None])
    coarse_chosen = jnp.where(is_hex, coarse_inv[0][None], coarse_inv[1][None])
    rows_iota = lax.broadcasted_iota(jnp.int32, (W, ELEMS), 0)
    valid_rows = (rows_iota < PRISM) | (element_kinds[None, :] == 0)
    start_field = jnp.where(valid_rows, initial, jnp.zeros_like(initial))
    decay_rate = jnp.exp(-damping)
    coarse_decay = jnp.exp(-COARSEN * damping)
    intervals = STEPS // COARSEN
    forcing_view = forcing.reshape(intervals, COARSEN, W, ELEMS)

    def fine_step(states_now, forcing_now):

        def single(paired):
            drive_term = decay_rate[None, :] * paired[0].astype(jnp.float32) + paired[1].astype(jnp.float32)
            return propagate(paired[0], drive_term, fine_chosen, coupling, tables)
        return lax.map(single, (states_now, forcing_now))
    zero_rest = jnp.zeros((intervals - 1, W, ELEMS), jnp.bfloat16)
    states_now = jnp.concatenate([start_field[None], zero_rest], axis=0)
    for step_index in range(COARSEN):
        states_now = fine_step(states_now, forcing_view[:, step_index])
    residuals = states_now

    def coarse_advance(carried, residual_now):
        drive_term = coarse_decay[None, :] * carried.astype(jnp.float32)
        propagated = propagate(carried, drive_term, coarse_chosen, coupling, tables)
        advanced = (propagated.astype(jnp.float32) + residual_now.astype(jnp.float32)).astype(jnp.bfloat16)
        return (advanced, advanced)
    _, coarse_values = lax.scan(coarse_advance, jnp.zeros((W, ELEMS), jnp.bfloat16), residuals)
    states_now = jnp.concatenate([start_field[None], coarse_values[:-1]], axis=0)
    produced = []
    for step_index in range(COARSEN - 1):
        states_now = fine_step(states_now, forcing_view[:, step_index])
        produced.append(states_now)
    produced.append(coarse_values)
    return jnp.stack(produced, axis=1).reshape(STEPS, W, ELEMS)
```

```python
import functools

import jax
import jax.numpy as jnp
from jax import lax
from jax.experimental import pallas as pl
from jax.experimental.pallas import tpu as pltpu
from jax.sharding import PartitionSpec as P

PRISM = 90
COARSEN = 4
LANES = 128
HALF = 64
ROWS = 144
FACES = 6
DEPTH = (FACES + 1) * ROWS
CHAIN = 4
OFFSETS = (1, -1, 2, -2)
MESH = pl.DeviceIdType.MESH
BF = jnp.bfloat16
F32 = jnp.float32


def matmul(left, right):
    return jnp.dot(left, right, preferred_element_type=F32)


def exact(left, right):
    return jnp.dot(left, right, preferred_element_type=F32, precision=lax.Precision.HIGHEST)


def kernel(
    spaces,
    windows,
    initial,
    forcing,
    meta,
    inverses,
    faces,
    out,
    source,
    received,
    gather_one,
    gather_two,
    pick,
    mats,
    own_mats,
    stacked,
    decay,
    drive,
    drive_sel,
    drive_left,
    drive_right,
    residual,
    meta_left,
    meta_right,
    send_sem,
    recv_sem,
    pass_send,
    pass_recv,
    meta_send,
    meta_recv,
    drive_send,
    drive_recv,
):
    place = lax.axis_index("space")
    window = lax.axis_index("tm")
    width = initial.shape[0]

    def inside(shift):
        return jnp.logical_and(place + shift >= 0, place + shift < spaces)

    source[0, 0:CHAIN] = jnp.zeros((CHAIN,) + source.shape[2:], BF)
    received[...] = jnp.zeros(received.shape, BF)
    drive_left[...] = jnp.zeros(drive_left.shape, BF)
    drive_right[...] = jnp.zeros(drive_right.shape, BF)
    meta_left[...] = jnp.zeros(meta_left.shape, F32)
    meta_right[...] = jnp.zeros(meta_right.shape, F32)

    barrier = pltpu.get_barrier_semaphore()
    for shift in OFFSETS:
        @pl.when(inside(shift))
        def _():
            pl.semaphore_signal(
                barrier,
                inc=1,
                device_id={"tm": window, "space": place + shift},
                device_id_type=MESH,
            )
    for shift in (0,) + OFFSETS:
        @pl.when(jnp.logical_and(inside(shift), window > 0))
        def _():
            pl.semaphore_signal(
                barrier,
                inc=1,
                device_id={"tm": window - 1, "space": place + shift},
                device_id_type=MESH,
            )
    beside_count = sum(jnp.where(inside(shift), 1, 0) for shift in OFFSETS)
    pl.semaphore_wait(
        barrier, beside_count + jnp.where(window < windows - 1, beside_count + 1, 0)
    )

    def meta_copy(side):
        shift = (1, -1)[side]
        return pltpu.make_async_remote_copy(
            src_ref=meta,
            dst_ref=(meta_left, meta_right)[side],
            send_sem=meta_send.at[side],
            recv_sem=meta_recv.at[side],
            device_id={"tm": window, "space": place + shift},
            device_id_type=MESH,
        )

    for side in range(2):
        @pl.when(inside((1, -1)[side]))
        def _():
            meta_copy(side).start()

    lane = lax.broadcasted_iota(jnp.int32, (1, LANES), 1)
    low = lane < HALF
    row_of = lax.broadcasted_iota(jnp.int32, (LANES, LANES), 0)
    send_own = meta[0:1, :].astype(jnp.int32)
    kind_own = meta[2:3, :]
    pick_own = (row_of == send_own).astype(F32)
    pick[...] = pick_own.astype(BF)

    drive[...] = jnp.zeros(drive.shape, BF)
    drive_sel[...] = jnp.zeros(drive_sel.shape, BF)

    def fill(index, carry):
        step, item = index // 4, index % 4
        drive[step, item, 0:width, :] = forcing[item * COARSEN + step]
        drive_sel[step, item] = matmul(drive[step, item], pick[...]).astype(BF)
        return carry

    lax.fori_loop(0, 16, fill, 0)

    def drive_copy(step, side):
        shift = (1, -1)[side]
        return pltpu.make_async_remote_copy(
            src_ref=drive_sel.at[step],
            dst_ref=(drive_left, drive_right)[side].at[step],
            send_sem=drive_send.at[step, side],
            recv_sem=drive_recv.at[step, side],
            device_id={"tm": window, "space": place + shift},
            device_id_type=MESH,
        )

    def state_copy(parity, slot, direction, target):
        return pltpu.make_async_remote_copy(
            src_ref=source.at[parity, slot, direction // 2],
            dst_ref=received.at[parity, slot, direction],
            send_sem=send_sem.at[parity, slot, direction],
            recv_sem=recv_sem.at[parity, slot, direction],
            device_id={"tm": target, "space": place + OFFSETS[direction]},
            device_id_type=MESH,
        )

    def pass_copy(part, target):
        return pltpu.make_async_remote_copy(
            src_ref=source.at[0, CHAIN, part],
            dst_ref=source.at[0, CHAIN, part],
            send_sem=pass_send.at[part],
            recv_sem=pass_recv.at[part],
            device_id={"tm": target, "space": place},
            device_id_type=MESH,
        )

    def send_state(parity, slot, target):
        for direction in range(4):
            @pl.when(inside(OFFSETS[direction]))
            def _():
                state_copy(parity, slot, direction, target).start()

    def await_state(parity, slot):
        for direction in range(4):
            @pl.when(inside(-OFFSETS[direction]))
            def _():
                state_copy(parity, slot, direction, window).wait_recv()

    def await_sent(parity, slot):
        for direction in range(4):
            @pl.when(inside(OFFSETS[direction]))
            def _():
                state_copy(parity, slot, direction, window).wait_send()

    for step in range(4):
        for side in range(2):
            @pl.when(inside((1, -1)[side]))
            def _():
                drive_copy(step, side).start()

    tall = lax.broadcasted_iota(jnp.int32, (width, LANES), 0)
    kept = jnp.logical_and(
        jnp.logical_or(tall < PRISM, kind_own < 0.5), jnp.broadcast_to(window, (1, 1)) == 0
    )
    source[0, 0, 0, 0:width, :] = jnp.where(kept, initial[...], jnp.zeros_like(initial))
    source[0, 0, 1] = matmul(source[0, 0, 0], pick[...]).astype(BF)

    @pl.when(window == 0)
    def _():
        send_state(0, 0, window)

    for index in range(4):
        mats[index] = matmul(inverses[index], faces[...]).astype(BF)
    for step in range(2):
        own_mats[step] = jnp.where(
            jnp.broadcast_to(meta[2:3, 0:1], (1, 1)) < 0.5, mats[2 * step], mats[2 * step + 1]
        )

    for side in range(2):
        @pl.when(inside((-1, 1)[side]))
        def _():
            meta_copy(side).wait_recv()
    for side in range(2):
        @pl.when(inside((1, -1)[side]))
        def _():
            meta_copy(side).wait_send()

    send_left = meta_left[0:1, :].astype(jnp.int32)
    send_right = meta_right[0:1, :].astype(jnp.int32)
    listed_left = exact(meta_left[...], (row_of == send_left).astype(F32))
    listed_right = exact(meta_right[...], (row_of == send_right).astype(F32))
    listed_own = exact(meta[...], pick_own)
    beside = jnp.where(low, listed_right, listed_left)
    there = jnp.where(
        low,
        jnp.broadcast_to(inside(1).astype(jnp.int32), (1, LANES)),
        jnp.broadcast_to(inside(-1).astype(jnp.int32), (1, LANES)),
    )
    for step in range(2):
        scale = -1.0 if step == 0 else -1.0 * COARSEN
        decay[step, 0:1, :] = jnp.exp(scale * meta[1:2, :])
        decay[step, 1:2, :] = jnp.exp(scale * beside[1:2, :]) * there.astype(F32)
        decay[step, 2:3, :] = jnp.exp(scale * listed_own[1:2, :])
    decay[0, 3:4, :] = kind_own
    decay[0, 4:5, :] = beside[2:3, :]

    def turned(row):
        return jnp.concatenate([row[:, HALF:], row[:, :HALF]], axis=1)

    own_map = jnp.concatenate(
        [LANES + lane, jnp.where(low, turned(send_left), 2 * LANES + turned(send_right))], axis=1
    )
    left_map = jnp.concatenate(
        [lane, jnp.where(low, 3 * LANES + HALF + lane, LANES + turned(send_own))], axis=1
    )
    right_map = jnp.concatenate(
        [2 * LANES + lane, jnp.where(low, LANES + turned(send_own), 3 * LANES + lane - HALF)], axis=1
    )
    filler = jnp.zeros((5, 2 * LANES), jnp.int32)
    maps = jnp.concatenate([own_map, left_map, right_map, filler], axis=0).astype(F32)
    code = lax.broadcasted_iota(jnp.int32, (2 * LANES, LANES), 0)
    spot = lax.broadcasted_iota(jnp.int32, (4 * LANES, LANES), 0)

    def whole(row):
        return (row + 0.5).astype(jnp.int32)

    def second(row):
        return jnp.where(row < LANES, row, jnp.where(row < LANES + HALF, row + HALF, row - HALF))

    for face in range(FACES):
        conn_own = whole(meta[8 + face : 9 + face, :])
        conn_beside = whole(beside[8 + face : 9 + face, :])
        conn_listed = whole(listed_own[8 + face : 9 + face, :])
        at_own = whole(exact(maps, (code == conn_own).astype(F32))[0:1, :])
        both = whole(exact(maps, (code == conn_beside).astype(F32)))
        at_beside = jnp.where(low, both[2:3, :], both[1:2, :])
        at_beside = jnp.where(there > 0, at_beside, -1)
        two_own = second(conn_own)
        two_listed = second(conn_listed)
        if face == FACES - 1:
            at_own = jnp.where(kind_own < 0.5, at_own, -1)
            two_own = jnp.where(kind_own < 0.5, two_own, -1)
            two_listed = jnp.where(kind_own < 0.5, two_listed, -1)
            at_beside = jnp.where(beside[2:3, :] < 0.5, at_beside, -1)
        here = slice(face * LANES, (face + 1) * LANES)
        after = slice((FACES + face) * LANES, (FACES + face + 1) * LANES)
        gather_one[:, here] = (spot == at_own).astype(F32).astype(BF)
        gather_one[:, after] = (spot == at_beside).astype(F32).astype(BF)
        gather_two[:, here] = (code == two_own).astype(F32).astype(BF)
        gather_two[:, after] = (code == two_listed).astype(F32).astype(BF)
    at_listed = jnp.where(low, 2 * LANES + send_right, send_left)
    at_listed = jnp.where(there > 0, at_listed, -1)
    gather_one[:, 2 * FACES * LANES :] = (spot == at_listed).astype(F32).astype(BF)

    residual[CHAIN] = jnp.zeros((ROWS, 2 * LANES), BF)

    def job(turn, item):
        early = turn < 4
        middle = jnp.logical_and(turn >= 4, turn < 8)
        coarse = jnp.logical_and(middle, item == 0)
        first = window == 0
        parity = jnp.where(middle, 0, turn % 2)
        slot = jnp.where(middle, turn, item)
        op = jnp.where(coarse, 1, 0)

        fresh = jnp.where(
            early,
            jnp.logical_or(turn >= 1, jnp.logical_and(item == 0, first)),
            jnp.logical_not(jnp.logical_and(middle, item == 1)),
        )
        handed = jnp.logical_and(turn == 4, item == 0)

        @pl.when(fresh)
        def _():
            await_state(parity, slot)

        @pl.when(jnp.logical_and(fresh, jnp.logical_not(handed)))
        def _():
            await_sent(parity, slot)

        @pl.when(handed)
        def _():
            for part in range(2):
                pass_copy(part, window).wait_recv()

        @pl.when(jnp.logical_and(early, item == 0))
        def _():
            for side in range(2):
                @pl.when(inside((-1, 1)[side]))
                def _():
                    drive_copy(turn, side).wait_recv()
            for side in range(2):
                @pl.when(inside((1, -1)[side]))
                def _():
                    drive_copy(turn, side).wait_send()

        fine_step = jnp.where(early, turn, jnp.where(middle, 0, turn - 7))
        fine_item = jnp.where(middle, turn - 4, item)
        drive_step = jnp.where(coarse, 4, fine_step)
        drive_item = jnp.where(coarse, 0, fine_item)
        drive_at = jnp.where(coarse, 0.0, 1.0)

        own = source[parity, slot, 0]
        listed = source[parity, slot, 1]
        outer = jnp.where(low, received[parity, slot, 3], received[parity, slot, 2])
        near = jnp.concatenate([received[parity, slot, 0], own], axis=1)
        far = jnp.concatenate([received[parity, slot, 1], outer], axis=1)
        decay_now = decay[op]
        drive_beside = jnp.where(
            low, drive_right[fine_step, fine_item], drive_left[fine_step, fine_item]
        )
        rhs_own = decay_now[0:1, :] * own.astype(F32) + drive_at * drive[
            fine_step, fine_item
        ].astype(F32)
        rhs_listed = decay_now[2:3, :] * listed.astype(F32) + drive_at * drive_sel[
            fine_step, fine_item
        ].astype(F32)

        def stack(gathered):
            gathered = gathered.astype(BF)
            for face in range(FACES):
                rows = slice(face * ROWS, (face + 1) * ROWS)
                stacked[rows, 0:LANES] = gathered[:, face * LANES : (face + 1) * LANES]
                stacked[rows, LANES : 2 * LANES] = gathered[
                    :, (FACES + face) * LANES : (FACES + face + 1) * LANES
                ]

        tail = slice(FACES * ROWS, DEPTH)
        gathered = matmul(near, gather_one[0 : 2 * LANES, :]) + matmul(
            far, gather_one[2 * LANES :, :]
        )
        stack(gathered)
        stacked[tail, 0:LANES] = rhs_own.astype(BF)
        rhs_beside = decay_now[1:2, :] * gathered[
            :, 2 * FACES * LANES :
        ] + drive_at * drive_beside.astype(F32)
        stacked[tail, LANES : 2 * LANES] = rhs_beside.astype(BF)
        kinds = jnp.concatenate([decay[0, 3:4, :], decay[0, 4:5, :]], axis=1)
        once = jnp.where(
            kinds < 0.5,
            matmul(mats[2 * op], stacked[...]),
            matmul(mats[2 * op + 1], stacked[...]),
        ).astype(BF)

        stack(matmul(once, gather_two[...]))
        stacked[tail, LANES : 2 * LANES] = rhs_listed.astype(BF)
        plus = residual[jnp.where(coarse, turn - 4, CHAIN)].astype(F32)
        twice = (matmul(own_mats[op], stacked[...]) + plus).astype(BF)

        leading = jnp.logical_and(first, item == 0)
        last_early = turn == 3

        @pl.when(last_early)
        def _():
            residual[item] = twice

        sending = jnp.where(
            early,
            jnp.logical_or(turn < 3, leading),
            jnp.where(
                coarse,
                jnp.logical_or(turn < 7, window < windows - 1),
                turn < 9,
            ),
        )
        fine = jnp.logical_and(middle, item == 1)
        out_slot = jnp.where(
            early,
            jnp.where(last_early, CHAIN + 1, item),
            jnp.where(
                coarse,
                jnp.where(turn == 7, CHAIN, turn + 1),
                jnp.where(fine, turn - 4, item),
            ),
        )
        out_parity = jnp.where(jnp.logical_or(middle, last_early), 0, (turn + 1) % 2)
        leaving = jnp.logical_and(coarse, turn == 7)
        target = jnp.where(leaving, window + 1, window)

        @pl.when(sending)
        def _():
            source[out_parity, out_slot, 0] = twice[:, 0:LANES]
            source[out_parity, out_slot, 1] = twice[:, LANES:]
            send_state(out_parity, out_slot, target)

            @pl.when(leaving)
            def _():
                for part in range(2):
                    pass_copy(part, target).start()

        out_index = jnp.where(
            early,
            turn,
            jnp.where(
                coarse,
                COARSEN * (turn - 4) + COARSEN - 1,
                jnp.where(fine, COARSEN * (turn - 4), COARSEN * item + turn - 7),
            ),
        )

        @pl.when(jnp.logical_or(jnp.logical_not(early), leading))
        def _():
            out[out_index] = twice[0:width, 0:LANES]

    def round_of(turn, carry):
        early = turn < 4
        middle = jnp.logical_and(turn >= 4, turn < 8)
        begin = jnp.where(jnp.logical_and(turn >= 8, window == 0), 1, 0)
        jobs = jnp.where(
            middle, jnp.where(jnp.logical_and(turn == 4, window == 0), 0, 2), 4
        )

        def one(item, inner):
            job(turn, item)
            return inner

        lax.fori_loop(begin, jobs, one, 0)
        return carry

    lax.fori_loop(0, 10, round_of, 0)

    @pl.when(window < windows - 1)
    def _():
        await_sent(0, CHAIN)
        for part in range(2):
            pass_copy(part, window + 1).wait_send()


def shards(initial, forcing, damping, block_inv, coarse_inv, coupling, etype, send_index, conn):
    width = initial.shape[0]
    steps = forcing.shape[0]
    spaces = lax.axis_size("space")
    windows = lax.axis_size("tm")
    grow = ROWS - width
    inverses = jnp.pad(
        jnp.concatenate([block_inv, coarse_inv], axis=0), ((0, 0), (0, grow), (0, grow))
    )
    unit = jnp.eye(ROWS, dtype=BF)[None]
    faces = jnp.concatenate([jnp.pad(-coupling, ((0, 0), (0, grow), (0, grow))), unit], axis=0)
    faces = faces.transpose(1, 0, 2).reshape(ROWS, DEPTH)
    meta = jnp.concatenate(
        [
            send_index.astype(F32)[None],
            damping[None],
            jnp.broadcast_to(etype.astype(F32)[:, None], (1, LANES)),
            jnp.zeros((5, LANES), F32),
            conn.astype(F32),
            jnp.zeros((2, LANES), F32),
        ],
        axis=0,
    )
    vmem = pl.BlockSpec(memory_space=pltpu.VMEM)
    dma = pltpu.SemaphoreType.DMA
    return pl.pallas_call(
        functools.partial(kernel, spaces, windows),
        out_shape=jax.ShapeDtypeStruct((steps, width, LANES), BF),
        in_specs=[vmem] * 5,
        out_specs=vmem,
        scratch_shapes=[
            pltpu.VMEM((2, 8, 2, ROWS, LANES), BF),
            pltpu.VMEM((2, 8, 4, ROWS, LANES), BF),
            pltpu.VMEM((4 * LANES, 13 * LANES), BF),
            pltpu.VMEM((2 * LANES, 12 * LANES), BF),
            pltpu.VMEM((LANES, LANES), BF),
            pltpu.VMEM((4, ROWS, DEPTH), BF),
            pltpu.VMEM((2, ROWS, DEPTH), BF),
            pltpu.VMEM((DEPTH, 2 * LANES), BF),
            pltpu.VMEM((2, 8, LANES), F32),
            pltpu.VMEM((4, 4, ROWS, LANES), BF),
            pltpu.VMEM((4, 4, ROWS, LANES), BF),
            pltpu.VMEM((4, 4, ROWS, LANES), BF),
            pltpu.VMEM((4, 4, ROWS, LANES), BF),
            pltpu.VMEM((5, ROWS, 2 * LANES), BF),
            pltpu.VMEM((16, LANES), F32),
            pltpu.VMEM((16, LANES), F32),
            dma((2, 8, 4)),
            dma((2, 8, 4)),
            dma((2,)),
            dma((2,)),
            dma((2,)),
            dma((2,)),
            dma((4, 2)),
            dma((4, 2)),
        ],
        compiler_params=pltpu.CompilerParams(
            collective_id=0, has_side_effects=True, vmem_limit_bytes=48 << 20
        ),
    )(initial, forcing, meta, inverses, faces)


def solution(mesh):
    in_specs = (
        P(None, "space"),
        P("tm", None, "space"),
        P("space"),
        P(),
        P(),
        P(),
        P("space"),
        P("space"),
        P(None, "space"),
    )
    out_specs = P("tm", None, "space")
    return jax.shard_map(shards, mesh=mesh, in_specs=in_specs, out_specs=out_specs, check_vma=False)
```

```python
import functools

import jax
import jax.numpy as jnp
from jax import lax
from jax.experimental import pallas as pl
from jax.experimental.pallas import tpu as pltpu
from jax.sharding import PartitionSpec as P

PRISM = 90
COARSEN = 4
LANES = 128
HALF = 64
ROWS = 144
FACES = 6
DEPTH = (FACES + 1) * ROWS
CHAIN = 4
GATED = 1
OFFSETS = (1, -1, 2, -2)
MESH = pl.DeviceIdType.MESH
BF = jnp.bfloat16
F32 = jnp.float32


def matmul(left, right):
    return jnp.dot(left, right, preferred_element_type=F32)


def take(table, index):
    return jnp.take_along_axis(table, index, axis=1, mode="promise_in_bounds")


def kernel(
    spaces,
    windows,
    initial_in,
    forcing_in,
    damping,
    block_in,
    coarse_in,
    coupling_in,
    etype,
    send_index,
    conn,
    out,
    initial,
    forcing,
    inverse,
    coupling,
    padded,
    faces,
    meta,
    source,
    received,
    gather_one,
    gather_two,
    pick,
    mats,
    own_mats,
    stacked,
    decay,
    drive,
    drive_sel,
    drive_out,
    drive_left,
    drive_right,
    residual,
    meta_left,
    meta_right,
    load_sem,
    send_sem,
    recv_sem,
    pass_send,
    pass_recv,
    meta_send,
    meta_recv,
    drive_send,
    drive_recv,
    gate,
):
    place = lax.axis_index("space")
    window = lax.axis_index("tm")
    width = initial.shape[0]

    def inside(shift):
        return jnp.logical_and(place + shift >= 0, place + shift < spaces)

    loads = [
        pltpu.make_async_copy(initial_in, initial, load_sem.at[0]),
        pltpu.make_async_copy(forcing_in, forcing, load_sem.at[1]),
        pltpu.make_async_copy(block_in, inverse.at[0:2], load_sem.at[2]),
        pltpu.make_async_copy(coarse_in, inverse.at[2:4], load_sem.at[3]),
        pltpu.make_async_copy(coupling_in, coupling, load_sem.at[4]),
    ]
    for load in loads:
        load.start()

    received[0, 0:CHAIN] = jnp.zeros((CHAIN,) + received.shape[2:], BF)

    @pl.when(jnp.logical_or(place < 2, place >= spaces - 2))
    def _():
        received[0, CHAIN:] = jnp.zeros((CHAIN,) + received.shape[2:], BF)
        received[1, 0:CHAIN] = jnp.zeros((CHAIN,) + received.shape[2:], BF)
        drive_left[...] = jnp.zeros(drive_left.shape, BF)
        drive_right[...] = jnp.zeros(drive_right.shape, BF)
        meta_left[...] = jnp.zeros(meta_left.shape, F32)
        meta_right[...] = jnp.zeros(meta_right.shape, F32)

    barrier = pltpu.get_barrier_semaphore()
    for shift in OFFSETS:
        @pl.when(inside(shift))
        def _():
            pl.semaphore_signal(
                barrier,
                inc=1,
                device_id={"tm": window, "space": place + shift},
                device_id_type=MESH,
            )
    for shift in (0,) + OFFSETS:
        @pl.when(jnp.logical_and(inside(shift), window > 0))
        def _():
            pl.semaphore_signal(
                barrier,
                inc=1,
                device_id={"tm": window - 1, "space": place + shift},
                device_id_type=MESH,
            )

    def meta_copy(side):
        shift = (1, -1)[side]
        return pltpu.make_async_remote_copy(
            src_ref=meta,
            dst_ref=(meta_left, meta_right)[side],
            send_sem=meta_send.at[side],
            recv_sem=meta_recv.at[side],
            device_id={"tm": window, "space": place + shift},
            device_id_type=MESH,
        )

    def drive_copy(step, side):
        shift = (1, -1)[side]
        return pltpu.make_async_remote_copy(
            src_ref=drive_out.at[side, step],
            dst_ref=(drive_left, drive_right)[side].at[step],
            send_sem=drive_send.at[step, side],
            recv_sem=drive_recv.at[step, side],
            device_id={"tm": window, "space": place + shift},
            device_id_type=MESH,
        )

    def state_copy(parity, slot, direction, target):
        return pltpu.make_async_remote_copy(
            src_ref=source.at[parity, slot, direction // 2],
            dst_ref=received.at[parity, slot, direction],
            send_sem=send_sem.at[parity, slot, direction],
            recv_sem=recv_sem.at[parity, slot, direction],
            device_id={"tm": target, "space": place + OFFSETS[direction]},
            device_id_type=MESH,
        )

    def pass_copy(part, target):
        return pltpu.make_async_remote_copy(
            src_ref=source.at[0, CHAIN, part],
            dst_ref=source.at[0, CHAIN, part],
            send_sem=pass_send.at[part],
            recv_sem=pass_recv.at[part],
            device_id={"tm": target, "space": place},
            device_id_type=MESH,
        )

    def send_state(parity, slot, target):
        for direction in range(4):
            @pl.when(inside(OFFSETS[direction]))
            def _():
                state_copy(parity, slot, direction, target).start()

    def await_state(parity, slot):
        for direction in range(4):
            @pl.when(inside(-OFFSETS[direction]))
            def _():
                state_copy(parity, slot, direction, window).wait_recv()

    def await_sent(parity, slot):
        for direction in range(4):
            @pl.when(inside(OFFSETS[direction]))
            def _():
                state_copy(parity, slot, direction, window).wait_send()

    def send_drive(step):
        for side in range(2):
            @pl.when(inside((1, -1)[side]))
            def _():
                drive_copy(step, side).start()

    def turned(row):
        return jnp.concatenate([row[:, HALF:], row[:, :HALF]], axis=1)

    def fill(step):
        def one(item, carry):
            drive[step, item, 0:width, :] = forcing[item * COARSEN + step]
            drive_sel[step, item] = matmul(drive[step, item], pick[...]).astype(BF)
            return carry

        lax.fori_loop(0, CHAIN, one, 0)
        for pair in range(2):
            even = drive_sel[step, 2 * pair]
            odd = turned(drive_sel[step, 2 * pair + 1])
            drive_out[0, step, pair] = jnp.where(low, odd, even)
            drive_out[1, step, pair] = jnp.where(low, even, odd)

    lane = lax.broadcasted_iota(jnp.int32, (1, LANES), 1)
    low = lane < HALF
    code = lax.broadcasted_iota(jnp.int32, (2 * LANES, LANES), 0)
    spot = lax.broadcasted_iota(jnp.int32, (4 * LANES, LANES), 0)

    meta[...] = jnp.zeros(meta.shape, F32)
    meta[0:1, :] = send_index[...].astype(F32)
    meta[1:2, :] = damping[...]
    meta[2:3, :] = jnp.broadcast_to(etype[...].astype(F32), (1, LANES))
    meta[8 : 8 + FACES, :] = conn[...].astype(F32)
    send_own = send_index[...]
    kind_own = meta[2:3, :]
    pick[...] = (code[0:LANES] == send_own).astype(F32).astype(BF)

    source[0, 0:CHAIN] = jnp.zeros((CHAIN,) + source.shape[2:], BF)
    tall = lax.broadcasted_iota(jnp.int32, (width, LANES), 0)
    kept = jnp.logical_and(
        jnp.logical_or(tall < PRISM, kind_own < 0.5), jnp.broadcast_to(window, (1, 1)) == 0
    )
    loads[0].wait()
    source[0, 0, 0, 0:width, :] = jnp.where(kept, initial[...], jnp.zeros_like(initial))
    source[0, 0, 1] = matmul(source[0, 0, 0], pick[...]).astype(BF)
    drive[:, :, LANES:, :] = jnp.zeros((CHAIN, CHAIN, ROWS - LANES, LANES), BF)
    loads[1].wait()
    fill(0)

    beside_count = sum(jnp.where(inside(shift), 1, 0) for shift in OFFSETS)
    pl.semaphore_wait(
        barrier, beside_count + jnp.where(window < windows - 1, beside_count + 1, 0)
    )
    for side in range(2):
        @pl.when(inside((1, -1)[side]))
        def _():
            meta_copy(side).start()

    @pl.when(window == 0)
    def _():
        send_state(0, 0, window)

    @pl.when(window % 2 == 0)
    def _():
        send_drive(0)

    for load in loads[2:]:
        load.wait()
    padded[...] = jnp.zeros(padded.shape, BF)
    padded[0:FACES, 0:width, 0:width] = -coupling[...]
    padded[FACES:, 0:width, 0:width] = inverse[...]
    across = lax.broadcasted_iota(jnp.int32, (ROWS, DEPTH), 1)
    down = lax.broadcasted_iota(jnp.int32, (ROWS, DEPTH), 0)
    placed = jnp.where(across == down + FACES * ROWS, 1.0, 0.0)
    for face in range(FACES):
        shifted = jnp.where(across == down + face * ROWS, 1.0, 0.0).astype(BF)
        placed = placed + matmul(padded[face], shifted)
    faces[...] = placed.astype(BF)
    for index in range(4):
        mats[index] = matmul(padded[FACES + index], faces[...]).astype(BF)
    for step in range(2):
        own_mats[step] = jnp.where(meta[2:3, 0:1] < 0.5, mats[2 * step], mats[2 * step + 1])

    def spread(row):
        return jnp.broadcast_to(row, (8, LANES))

    def whole(rows):
        return (rows + 0.5).astype(jnp.int32)

    def onehot(rows, index):
        return (rows == index).astype(F32).astype(BF)

    def located(codes, start, listed_at):
        past = jnp.maximum(codes - LANES, 0)
        return jnp.where(codes < LANES, start + codes, take(spread(listed_at), past))

    def second(codes):
        return jnp.where(
            codes < LANES, codes, jnp.where(codes < LANES + HALF, codes + HALF, codes - HALF)
        )

    last_face = lax.broadcasted_iota(jnp.int32, (8, LANES), 0) == FACES - 1

    def masked(index, kind):
        return jnp.where(jnp.logical_and(last_face, kind > 0.5), -1, index)

    conn_own = whole(meta[8:16, :])
    damp_listed = take(meta[0:8, :], spread(send_own))[1:2, :]
    two_own = masked(second(conn_own), kind_own)
    two_listed = masked(second(take(conn_own, spread(send_own))), kind_own)
    for face in range(FACES):
        here = slice(face * LANES, (face + 1) * LANES)
        after = slice((FACES + face) * LANES, (FACES + face + 1) * LANES)
        gather_two[:, here] = onehot(code, two_own[face : face + 1, :])
        gather_two[:, after] = onehot(code, two_listed[face : face + 1, :])

    for side in range(2):
        @pl.when(inside((-1, 1)[side]))
        def _():
            meta_copy(side).wait_recv()
    for side in range(2):
        @pl.when(inside((1, -1)[side]))
        def _():
            meta_copy(side).wait_send()

    send_left = whole(meta_left[0:1, :])
    send_right = whole(meta_right[0:1, :])
    conn_left = whole(take(meta_left[8:16, :], spread(send_left)))
    conn_right = whole(take(meta_right[8:16, :], spread(send_right)))
    damp_left = take(meta_left[0:8, :], spread(send_left))[1:2, :]
    damp_right = take(meta_right[0:8, :], spread(send_right))[1:2, :]
    damp_beside = jnp.where(low, damp_right, damp_left)
    kind_beside = jnp.where(low, meta_right[2:3, :], meta_left[2:3, :])
    there = jnp.where(
        low,
        jnp.broadcast_to(inside(1).astype(jnp.int32), (1, LANES)),
        jnp.broadcast_to(inside(-1).astype(jnp.int32), (1, LANES)),
    )
    for step in range(2):
        scale = -1.0 if step == 0 else -1.0 * COARSEN
        decay[step, 0:1, :] = jnp.exp(scale * meta[1:2, :])
        decay[step, 1:2, :] = jnp.exp(scale * damp_beside) * there.astype(F32)
        decay[step, 2:3, :] = jnp.exp(scale * damp_listed)
    decay[0, 3:4, :] = kind_own
    decay[0, 4:5, :] = kind_beside

    at_own = located(
        conn_own, LANES, jnp.where(low, turned(send_left), 2 * LANES + turned(send_right))
    )
    at_left = located(
        conn_left, 0, jnp.where(low, 3 * LANES + HALF + lane, LANES + turned(send_own))
    )
    at_right = located(
        conn_right,
        2 * LANES,
        jnp.where(low, LANES + turned(send_own), 3 * LANES + lane - HALF),
    )
    at_own = masked(at_own, kind_own)
    at_beside = masked(jnp.where(low, at_right, at_left), kind_beside)
    at_beside = jnp.where(there > 0, at_beside, -1)
    for face in range(FACES):
        here = slice(face * LANES, (face + 1) * LANES)
        after = slice((FACES + face) * LANES, (FACES + face + 1) * LANES)
        gather_one[:, here] = onehot(spot, at_own[face : face + 1, :])
        gather_one[:, after] = onehot(spot, at_beside[face : face + 1, :])
    at_listed = jnp.where(low, 2 * LANES + send_right, send_left)
    at_listed = jnp.where(there > 0, at_listed, -1)
    gather_one[:, 2 * FACES * LANES :] = onehot(spot, at_listed)

    residual[CHAIN] = jnp.zeros((ROWS, 2 * LANES), BF)

    @pl.when(window % 2 == 1)
    def _():
        pl.semaphore_wait(gate, 1)
        send_drive(0)


    def job(turn, item):
        early = turn < 4
        middle = jnp.logical_and(turn >= 4, turn < 8)
        ending = jnp.logical_and(turn == 7, window == windows - 1)
        fine = jnp.logical_and(middle, item == jnp.where(ending, 0, 1))
        coarse = jnp.logical_and(middle, jnp.logical_not(fine))
        first = window == 0
        parity = jnp.where(middle, 0, turn % 2)
        slot = jnp.where(middle, turn, item)
        op = jnp.where(coarse, 1, 0)

        fresh = jnp.where(
            early,
            jnp.logical_or(turn >= 1, jnp.logical_and(item == 0, first)),
            jnp.logical_not(jnp.logical_and(middle, item == 1)),
        )
        handed = jnp.logical_and(turn == 4, item == 0)

        @pl.when(fresh)
        def _():
            await_state(parity, slot)

        @pl.when(jnp.logical_and(fresh, jnp.logical_not(handed)))
        def _():
            await_sent(parity, slot)

        @pl.when(handed)
        def _():
            for part in range(2):
                pass_copy(part, window).wait_recv()

        @pl.when(jnp.logical_and(early, item == 0))
        def _():
            for side in range(2):
                @pl.when(inside((-1, 1)[side]))
                def _():
                    drive_copy(turn, side).wait_recv()
            for side in range(2):
                @pl.when(inside((1, -1)[side]))
                def _():
                    drive_copy(turn, side).wait_send()

        fine_step = jnp.where(early, turn, jnp.where(middle, 0, turn - 7))
        fine_item = jnp.where(middle, turn - 4, item)
        drive_step = jnp.where(coarse, 4, fine_step)
        drive_item = jnp.where(coarse, 0, fine_item)
        drive_at = jnp.where(coarse, 0.0, 1.0)

        own = source[parity, slot, 0]
        listed = source[parity, slot, 1]
        outer = jnp.where(low, received[parity, slot, 3], received[parity, slot, 2])
        near = jnp.concatenate([received[parity, slot, 0], own], axis=1)
        far = jnp.concatenate([received[parity, slot, 1], outer], axis=1)
        decay_now = decay[op]
        from_left = drive_left[fine_step, fine_item // 2]
        from_right = drive_right[fine_step, fine_item // 2]
        drive_beside = jnp.where(
            jnp.broadcast_to(fine_item % 2, (1, 1)) == 0,
            jnp.where(low, from_right, from_left),
            turned(jnp.where(low, from_left, from_right)),
        )
        rhs_own = decay_now[0:1, :] * own.astype(F32) + drive_at * drive[
            fine_step, fine_item
        ].astype(F32)
        rhs_listed = decay_now[2:3, :] * listed.astype(F32) + drive_at * drive_sel[
            fine_step, fine_item
        ].astype(F32)

        def stack(gathered):
            gathered = gathered.astype(BF)
            for face in range(FACES):
                rows = slice(face * ROWS, (face + 1) * ROWS)
                stacked[rows, 0:LANES] = gathered[:, face * LANES : (face + 1) * LANES]
                stacked[rows, LANES : 2 * LANES] = gathered[
                    :, (FACES + face) * LANES : (FACES + face + 1) * LANES
                ]

        tail = slice(FACES * ROWS, DEPTH)
        gathered = matmul(near, gather_one[0 : 2 * LANES, :]) + matmul(
            far, gather_one[2 * LANES :, :]
        )
        stack(gathered)
        stacked[tail, 0:LANES] = rhs_own.astype(BF)
        rhs_beside = decay_now[1:2, :] * gathered[
            :, 2 * FACES * LANES :
        ] + drive_at * drive_beside.astype(F32)
        stacked[tail, LANES : 2 * LANES] = rhs_beside.astype(BF)
        kinds = jnp.concatenate([decay[0, 3:4, :], decay[0, 4:5, :]], axis=1)
        once = jnp.where(
            kinds < 0.5,
            matmul(mats[2 * op], stacked[...]),
            matmul(mats[2 * op + 1], stacked[...]),
        ).astype(BF)

        stack(matmul(once, gather_two[...]))
        stacked[tail, LANES : 2 * LANES] = rhs_listed.astype(BF)
        plus = residual[jnp.where(coarse, turn - 4, CHAIN)].astype(F32)
        twice = (matmul(own_mats[op], stacked[...]) + plus).astype(BF)

        leading = jnp.logical_and(first, item == 0)
        last_early = turn == 3

        @pl.when(last_early)
        def _():
            residual[item] = twice

        sending = jnp.where(
            early,
            jnp.logical_or(turn < 3, leading),
            jnp.where(
                coarse,
                jnp.logical_or(turn < 7, window < windows - 1),
                turn < 9,
            ),
        )
        out_slot = jnp.where(
            early,
            jnp.where(last_early, CHAIN + 1, item),
            jnp.where(
                coarse,
                jnp.where(turn == 7, CHAIN, turn + 1),
                jnp.where(fine, turn - 4, item),
            ),
        )
        out_parity = jnp.where(jnp.logical_or(middle, last_early), 0, (turn + 1) % 2)
        leaving = jnp.logical_and(coarse, turn == 7)
        target = jnp.where(leaving, window + 1, window)

        @pl.when(sending)
        def _():
            source[out_parity, out_slot, 0] = twice[:, 0:LANES]
            source[out_parity, out_slot, 1] = twice[:, LANES:]
            send_state(out_parity, out_slot, target)

            @pl.when(leaving)
            def _():
                for part in range(2):
                    pass_copy(part, target).start()

        out_index = jnp.where(
            early,
            turn,
            jnp.where(
                coarse,
                COARSEN * (turn - 4) + COARSEN - 1,
                jnp.where(fine, COARSEN * (turn - 4), COARSEN * item + turn - 7),
            ),
        )

        @pl.when(jnp.logical_or(jnp.logical_not(early), leading))
        def _():
            out[out_index] = twice[0:width, 0:LANES]

    def round_of(turn, carry):
        early = turn < 4
        middle = jnp.logical_and(turn >= 4, turn < 8)
        begin = jnp.where(jnp.logical_and(turn >= 8, window == 0), 1, 0)
        jobs = jnp.where(
            middle, jnp.where(jnp.logical_and(turn == 4, window == 0), 0, 2), 4
        )

        def one(item, inner):
            job(turn, item)

            @pl.when(jnp.logical_and(turn < 3, item == 1))
            def _():
                fill(turn + 1)
                send_drive(turn + 1)

            @pl.when(
                jnp.logical_and(
                    jnp.logical_and(turn == GATED, item == 3), window % 2 == 0
                )
            )
            def _():
                pl.semaphore_signal(
                    gate,
                    inc=1,
                    device_id={"tm": window + 1, "space": place},
                    device_id_type=MESH,
                )

            return inner

        lax.fori_loop(begin, jobs, one, 0)
        return carry

    lax.fori_loop(0, 10, round_of, 0)

    @pl.when(window < windows - 1)
    def _():
        await_sent(0, CHAIN)
        for part in range(2):
            pass_copy(part, window + 1).wait_send()


def shards(initial, forcing, damping, block_inv, coarse_inv, coupling, etype, send_index, conn):
    width = initial.shape[0]
    steps = forcing.shape[0]
    spaces = lax.axis_size("space")
    windows = lax.axis_size("tm")
    vmem = pl.BlockSpec(memory_space=pltpu.VMEM)
    far = pl.BlockSpec(memory_space=pl.ANY)
    dma = pltpu.SemaphoreType.DMA
    return pl.pallas_call(
        functools.partial(kernel, spaces, windows),
        out_shape=jax.ShapeDtypeStruct((steps, width, LANES), BF),
        in_specs=[far, far, vmem, far, far, far, vmem, vmem, vmem],
        out_specs=vmem,
        scratch_shapes=[
            pltpu.VMEM((width, LANES), BF),
            pltpu.VMEM((steps, width, LANES), BF),
            pltpu.VMEM((4, width, width), BF),
            pltpu.VMEM((FACES, width, width), BF),
            pltpu.VMEM((FACES + 4, ROWS, ROWS), BF),
            pltpu.VMEM((ROWS, DEPTH), BF),
            pltpu.VMEM((16, LANES), F32),
            pltpu.VMEM((2, 8, 2, ROWS, LANES), BF),
            pltpu.VMEM((2, 8, 4, ROWS, LANES), BF),
            pltpu.VMEM((4 * LANES, 13 * LANES), BF),
            pltpu.VMEM((2 * LANES, 12 * LANES), BF),
            pltpu.VMEM((LANES, LANES), BF),
            pltpu.VMEM((4, ROWS, DEPTH), BF),
            pltpu.VMEM((2, ROWS, DEPTH), BF),
            pltpu.VMEM((DEPTH, 2 * LANES), BF),
            pltpu.VMEM((2, 8, LANES), F32),
            pltpu.VMEM((4, 4, ROWS, LANES), BF),
            pltpu.VMEM((4, 4, ROWS, LANES), BF),
            pltpu.VMEM((2, 4, 2, ROWS, LANES), BF),
            pltpu.VMEM((4, 2, ROWS, LANES), BF),
            pltpu.VMEM((4, 2, ROWS, LANES), BF),
            pltpu.VMEM((5, ROWS, 2 * LANES), BF),
            pltpu.VMEM((16, LANES), F32),
            pltpu.VMEM((16, LANES), F32),
            dma((5,)),
            dma((2, 8, 4)),
            dma((2, 8, 4)),
            dma((2,)),
            dma((2,)),
            dma((2,)),
            dma((2,)),
            dma((4, 2)),
            dma((4, 2)),
            pltpu.SemaphoreType.REGULAR,
        ],
        compiler_params=pltpu.CompilerParams(
            collective_id=0, has_side_effects=True, vmem_limit_bytes=48 << 20
        ),
    )(
        initial,
        forcing,
        damping[None],
        block_inv,
        coarse_inv,
        coupling,
        etype[None],
        send_index[None],
        conn,
    )


def solution(mesh):
    in_specs = (
        P(None, "space"),
        P("tm", None, "space"),
        P("space"),
        P(),
        P(),
        P(),
        P("space"),
        P("space"),
        P(None, "space"),
    )
    out_specs = P("tm", None, "space")
    return jax.shard_map(shards, mesh=mesh, in_specs=in_specs, out_specs=out_specs, check_vma=False)
```

```python
import functools

import jax
import jax.numpy as jnp
from jax import lax
from jax.experimental import pallas as pl
from jax.experimental.pallas import tpu as pltpu
from jax.sharding import PartitionSpec as P

PRISM = 90
COARSEN = 4
LANES = 128
HALF = 64
ROWS = 144
FACES = 6
DEPTH = (FACES + 1) * ROWS
CHAIN = 4
GATED = 1
OFFSETS = (1, -1, 2, -2)
MESH = pl.DeviceIdType.MESH
BF = jnp.bfloat16
F32 = jnp.float32


def matmul(left, right):
    return jnp.dot(left, right, preferred_element_type=F32)


def take(table, index):
    return jnp.take_along_axis(table, index, axis=1, mode="promise_in_bounds")


def kernel(
    spaces,
    windows,
    initial_in,
    forcing_in,
    damping,
    inverse_in,
    coupling_in,
    etype,
    send_index,
    conn,
    out,
    initial,
    forcing,
    inverse,
    coupling,
    padded,
    faces,
    meta,
    source,
    received,
    gather_one,
    gather_two,
    pick,
    mats,
    own_mats,
    stacked,
    waiting,
    decay,
    drive,
    drive_sel,
    drive_out,
    drive_left,
    drive_right,
    residual,
    meta_left,
    meta_right,
    load_sem,
    send_sem,
    recv_sem,
    pass_send,
    pass_recv,
    meta_send,
    meta_recv,
    drive_send,
    drive_recv,
    gate,
):
    place = lax.axis_index("space")
    window = lax.axis_index("tm")
    width = initial.shape[0]

    def inside(shift):
        return jnp.logical_and(place + shift >= 0, place + shift < spaces)

    loads = [
        pltpu.make_async_copy(initial_in, initial, load_sem.at[0]),
        pltpu.make_async_copy(forcing_in, forcing, load_sem.at[1]),
        pltpu.make_async_copy(inverse_in, inverse, load_sem.at[2]),
        pltpu.make_async_copy(coupling_in, coupling, load_sem.at[3]),
    ]
    for load in loads:
        load.start()

    received[0, 0:CHAIN] = jnp.zeros((CHAIN,) + received.shape[2:], BF)

    @pl.when(jnp.logical_or(place < 2, place >= spaces - 2))
    def _():
        received[0, CHAIN:] = jnp.zeros((CHAIN,) + received.shape[2:], BF)
        received[1, 0:CHAIN] = jnp.zeros((CHAIN,) + received.shape[2:], BF)
        drive_left[...] = jnp.zeros(drive_left.shape, BF)
        drive_right[...] = jnp.zeros(drive_right.shape, BF)
        meta_left[...] = jnp.zeros(meta_left.shape, F32)
        meta_right[...] = jnp.zeros(meta_right.shape, F32)

    barrier = pltpu.get_barrier_semaphore()
    for shift in OFFSETS:
        @pl.when(inside(shift))
        def _():
            pl.semaphore_signal(
                barrier,
                inc=1,
                device_id={"tm": window, "space": place + shift},
                device_id_type=MESH,
            )
    for shift in (0,) + OFFSETS:
        @pl.when(jnp.logical_and(inside(shift), window > 0))
        def _():
            pl.semaphore_signal(
                barrier,
                inc=1,
                device_id={"tm": window - 1, "space": place + shift},
                device_id_type=MESH,
            )

    def meta_copy(side):
        shift = (1, -1)[side]
        return pltpu.make_async_remote_copy(
            src_ref=meta,
            dst_ref=(meta_left, meta_right)[side],
            send_sem=meta_send.at[side],
            recv_sem=meta_recv.at[side],
            device_id={"tm": window, "space": place + shift},
            device_id_type=MESH,
        )

    def drive_copy(step, side):
        shift = (1, -1)[side]
        return pltpu.make_async_remote_copy(
            src_ref=drive_out.at[side, step],
            dst_ref=(drive_left, drive_right)[side].at[step],
            send_sem=drive_send.at[step, side],
            recv_sem=drive_recv.at[step, side],
            device_id={"tm": window, "space": place + shift},
            device_id_type=MESH,
        )

    def state_copy(parity, slot, direction, target):
        return pltpu.make_async_remote_copy(
            src_ref=source.at[parity, slot, direction // 2],
            dst_ref=received.at[parity, slot, direction],
            send_sem=send_sem.at[parity, slot, direction],
            recv_sem=recv_sem.at[parity, slot, direction],
            device_id={"tm": target, "space": place + OFFSETS[direction]},
            device_id_type=MESH,
        )

    def pass_copy(part, target):
        return pltpu.make_async_remote_copy(
            src_ref=source.at[0, CHAIN, part],
            dst_ref=source.at[0, CHAIN, part],
            send_sem=pass_send.at[part],
            recv_sem=pass_recv.at[part],
            device_id={"tm": target, "space": place},
            device_id_type=MESH,
        )

    def send_state(parity, slot, target):
        for direction in range(4):
            @pl.when(inside(OFFSETS[direction]))
            def _():
                state_copy(parity, slot, direction, target).start()

    def await_state(parity, slot):
        for direction in range(4):
            @pl.when(inside(-OFFSETS[direction]))
            def _():
                state_copy(parity, slot, direction, window).wait_recv()

    def await_sent(parity, slot):
        for direction in range(4):
            @pl.when(inside(OFFSETS[direction]))
            def _():
                state_copy(parity, slot, direction, window).wait_send()

    def send_drive(step):
        for side in range(2):
            @pl.when(inside((1, -1)[side]))
            def _():
                drive_copy(step, side).start()

    def turned(row):
        return jnp.concatenate([row[:, HALF:], row[:, :HALF]], axis=1)

    def fill(step):
        def one(item, carry):
            drive[step, item, 0:width, :] = forcing[item * COARSEN + step]
            drive_sel[step, item] = matmul(drive[step, item], pick[...]).astype(BF)
            return carry

        lax.fori_loop(0, CHAIN, one, 0)
        for pair in range(2):
            even = drive_sel[step, 2 * pair]
            odd = turned(drive_sel[step, 2 * pair + 1])
            drive_out[0, step, pair] = jnp.where(low, odd, even)
            drive_out[1, step, pair] = jnp.where(low, even, odd)

    lane = lax.broadcasted_iota(jnp.int32, (1, LANES), 1)
    low = lane < HALF
    code = lax.broadcasted_iota(jnp.int32, (2 * LANES, LANES), 0)
    spot = lax.broadcasted_iota(jnp.int32, (4 * LANES, LANES), 0)

    meta[...] = jnp.zeros(meta.shape, F32)
    meta[0:1, :] = send_index[...].astype(F32)
    meta[1:2, :] = damping[...]
    meta[2:3, :] = jnp.broadcast_to(etype[...].astype(F32), (1, LANES))
    meta[8 : 8 + FACES, :] = conn[...].astype(F32)
    send_own = send_index[...]
    kind_own = meta[2:3, :]
    pick[...] = (code[0:LANES] == send_own).astype(F32).astype(BF)

    source[0, 0:CHAIN] = jnp.zeros((CHAIN,) + source.shape[2:], BF)
    tall = lax.broadcasted_iota(jnp.int32, (width, LANES), 0)
    kept = jnp.logical_and(
        jnp.logical_or(tall < PRISM, kind_own < 0.5), jnp.broadcast_to(window, (1, 1)) == 0
    )
    loads[0].wait()
    source[0, 0, 0, 0:width, :] = jnp.where(kept, initial[...], jnp.zeros_like(initial))
    source[0, 0, 1] = matmul(source[0, 0, 0], pick[...]).astype(BF)
    drive[:, :, LANES:, :] = jnp.zeros((CHAIN, CHAIN, ROWS - LANES, LANES), BF)
    loads[1].wait()
    fill(0)

    beside_count = sum(jnp.where(inside(shift), 1, 0) for shift in OFFSETS)
    pl.semaphore_wait(
        barrier, beside_count + jnp.where(window < windows - 1, beside_count + 1, 0)
    )
    for side in range(2):
        @pl.when(inside((1, -1)[side]))
        def _():
            meta_copy(side).start()

    @pl.when(window == 0)
    def _():
        send_state(0, 0, window)

    @pl.when(window % 2 == 0)
    def _():
        send_drive(0)

    for load in loads[2:]:
        load.wait()
    padded[...] = jnp.zeros(padded.shape, BF)
    padded[0:FACES, 0:width, 0:width] = -coupling[...]
    padded[FACES:, 0:width, 0:width] = inverse[...]
    across = lax.broadcasted_iota(jnp.int32, (ROWS, DEPTH), 1)
    down = lax.broadcasted_iota(jnp.int32, (ROWS, DEPTH), 0)
    placed = jnp.where(across == down + FACES * ROWS, 1.0, 0.0)
    for face in range(FACES):
        shifted = jnp.where(across == down + face * ROWS, 1.0, 0.0).astype(BF)
        placed = placed + matmul(padded[face], shifted)
    faces[...] = placed.astype(BF)
    for index in range(4):
        mats[index] = matmul(padded[FACES + index], faces[...]).astype(BF)
    for step in range(2):
        own_mats[step] = jnp.where(meta[2:3, 0:1] < 0.5, mats[2 * step], mats[2 * step + 1])

    def spread(row):
        return jnp.broadcast_to(row, (8, LANES))

    def whole(rows):
        return (rows + 0.5).astype(jnp.int32)

    def onehot(rows, index):
        return (rows == index).astype(F32).astype(BF)

    def located(codes, start, listed_at):
        past = jnp.maximum(codes - LANES, 0)
        return jnp.where(codes < LANES, start + codes, take(spread(listed_at), past))

    def second(codes):
        return jnp.where(
            codes < LANES, codes, jnp.where(codes < LANES + HALF, codes + HALF, codes - HALF)
        )

    last_face = lax.broadcasted_iota(jnp.int32, (8, LANES), 0) == FACES - 1

    def masked(index, kind):
        return jnp.where(jnp.logical_and(last_face, kind > 0.5), -1, index)

    conn_own = whole(meta[8:16, :])
    damp_listed = take(meta[0:8, :], spread(send_own))[1:2, :]
    two_own = masked(second(conn_own), kind_own)
    two_listed = masked(second(take(conn_own, spread(send_own))), kind_own)
    for face in range(FACES):
        here = slice(face * LANES, (face + 1) * LANES)
        after = slice((FACES + face) * LANES, (FACES + face + 1) * LANES)
        gather_two[:, here] = onehot(code, two_own[face : face + 1, :])
        gather_two[:, after] = onehot(code, two_listed[face : face + 1, :])

    for step in range(1, 4):
        fill(step)

    for side in range(2):
        @pl.when(inside((-1, 1)[side]))
        def _():
            meta_copy(side).wait_recv()
    for side in range(2):
        @pl.when(inside((1, -1)[side]))
        def _():
            meta_copy(side).wait_send()

    send_left = whole(meta_left[0:1, :])
    send_right = whole(meta_right[0:1, :])
    conn_left = whole(take(meta_left[8:16, :], spread(send_left)))
    conn_right = whole(take(meta_right[8:16, :], spread(send_right)))
    damp_left = take(meta_left[0:8, :], spread(send_left))[1:2, :]
    damp_right = take(meta_right[0:8, :], spread(send_right))[1:2, :]
    damp_beside = jnp.where(low, damp_right, damp_left)
    kind_beside = jnp.where(low, meta_right[2:3, :], meta_left[2:3, :])
    there = jnp.where(
        low,
        jnp.broadcast_to(inside(1).astype(jnp.int32), (1, LANES)),
        jnp.broadcast_to(inside(-1).astype(jnp.int32), (1, LANES)),
    )
    for step in range(2):
        scale = -1.0 if step == 0 else -1.0 * COARSEN
        decay[step, 0:1, :] = jnp.exp(scale * meta[1:2, :])
        decay[step, 1:2, :] = jnp.exp(scale * damp_beside) * there.astype(F32)
        decay[step, 2:3, :] = jnp.exp(scale * damp_listed)
    decay[0, 3:4, :] = kind_own
    decay[0, 4:5, :] = kind_beside

    at_own = located(
        conn_own, LANES, jnp.where(low, turned(send_left), 2 * LANES + turned(send_right))
    )
    at_left = located(
        conn_left, 0, jnp.where(low, 3 * LANES + HALF + lane, LANES + turned(send_own))
    )
    at_right = located(
        conn_right,
        2 * LANES,
        jnp.where(low, LANES + turned(send_own), 3 * LANES + lane - HALF),
    )
    at_own = masked(at_own, kind_own)
    at_beside = masked(jnp.where(low, at_right, at_left), kind_beside)
    at_beside = jnp.where(there > 0, at_beside, -1)
    for face in range(FACES):
        here = slice(face * LANES, (face + 1) * LANES)
        after = slice((FACES + face) * LANES, (FACES + face + 1) * LANES)
        gather_one[:, here] = onehot(spot, at_own[face : face + 1, :])
        gather_one[:, after] = onehot(spot, at_beside[face : face + 1, :])
    at_listed = jnp.where(low, 2 * LANES + send_right, send_left)
    at_listed = jnp.where(there > 0, at_listed, -1)
    gather_one[:, 2 * FACES * LANES :] = onehot(spot, at_listed)

    residual[CHAIN] = jnp.zeros((ROWS, 2 * LANES), BF)

    @pl.when(window % 2 == 1)
    def _():
        pl.semaphore_wait(gate, 1)
        send_drive(0)


    def job(turn, item):
        early = turn < 4
        middle = jnp.logical_and(turn >= 4, turn < 8)
        ending = jnp.logical_and(turn == 7, window == windows - 1)
        fine = jnp.logical_and(middle, item == jnp.where(ending, 0, 1))
        coarse = jnp.logical_and(middle, jnp.logical_not(fine))
        first = window == 0
        parity = jnp.where(middle, 0, turn % 2)
        slot = jnp.where(middle, turn, item)
        op = jnp.where(coarse, 1, 0)

        fresh = jnp.where(
            early,
            jnp.logical_or(turn >= 1, jnp.logical_and(item == 0, first)),
            jnp.logical_not(jnp.logical_and(middle, item == 1)),
        )
        handed = jnp.logical_and(turn == 4, item == 0)

        @pl.when(handed)
        def _():
            for part in range(2):
                pass_copy(part, window).wait_recv()

        @pl.when(jnp.logical_and(early, item == 0))
        def _():
            for side in range(2):
                @pl.when(inside((-1, 1)[side]))
                def _():
                    drive_copy(turn, side).wait_recv()
            for side in range(2):
                @pl.when(inside((1, -1)[side]))
                def _():
                    drive_copy(turn, side).wait_send()

        fine_step = jnp.where(early, turn, jnp.where(middle, 0, turn - 7))
        fine_item = jnp.where(middle, turn - 4, item)
        drive_step = jnp.where(coarse, 4, fine_step)
        drive_item = jnp.where(coarse, 0, fine_item)
        drive_at = jnp.where(coarse, 0.0, 1.0)

        own = source[parity, slot, 0]
        listed = source[parity, slot, 1]
        decay_now = decay[op]
        from_left = drive_left[fine_step, fine_item // 2]
        from_right = drive_right[fine_step, fine_item // 2]
        drive_beside = jnp.where(
            jnp.broadcast_to(fine_item % 2, (1, 1)) == 0,
            jnp.where(low, from_right, from_left),
            turned(jnp.where(low, from_left, from_right)),
        )
        rhs_own = decay_now[0:1, :] * own.astype(F32) + drive_at * drive[
            fine_step, fine_item
        ].astype(F32)
        rhs_listed = decay_now[2:3, :] * listed.astype(F32) + drive_at * drive_sel[
            fine_step, fine_item
        ].astype(F32)

        def stack(gathered):
            gathered = gathered.astype(BF)
            for face in range(FACES):
                rows = slice(face * ROWS, (face + 1) * ROWS)
                stacked[rows, 0:LANES] = gathered[:, face * LANES : (face + 1) * LANES]
                stacked[rows, LANES : 2 * LANES] = gathered[
                    :, (FACES + face) * LANES : (FACES + face + 1) * LANES
                ]

        tail = slice(FACES * ROWS, DEPTH)
        stacked[tail, 0:LANES] = rhs_own.astype(BF)
        waiting[0] = rhs_listed.astype(BF)
        waiting[1] = (drive_at * drive_beside.astype(F32)).astype(BF)

        @pl.when(fresh)
        def _():
            await_state(parity, slot)

        outer = jnp.where(low, received[parity, slot, 3], received[parity, slot, 2])
        near = jnp.concatenate([received[parity, slot, 0], own], axis=1)
        far = jnp.concatenate([received[parity, slot, 1], outer], axis=1)
        gathered = matmul(near, gather_one[0 : 2 * LANES, :]) + matmul(
            far, gather_one[2 * LANES :, :]
        )
        stack(gathered)
        rhs_beside = decay_now[1:2, :] * gathered[
            :, 2 * FACES * LANES :
        ] + waiting[1].astype(F32)
        stacked[tail, LANES : 2 * LANES] = rhs_beside.astype(BF)
        kinds = jnp.concatenate([decay[0, 3:4, :], decay[0, 4:5, :]], axis=1)
        once = jnp.where(
            kinds < 0.5,
            matmul(mats[2 * op], stacked[...]),
            matmul(mats[2 * op + 1], stacked[...]),
        ).astype(BF)

        stack(matmul(once, gather_two[...]))
        stacked[tail, LANES : 2 * LANES] = waiting[0]
        plus = residual[jnp.where(coarse, turn - 4, CHAIN)].astype(F32)
        twice = (matmul(own_mats[op], stacked[...]) + plus).astype(BF)

        leading = jnp.logical_and(first, item == 0)
        last_early = turn == 3

        @pl.when(last_early)
        def _():
            residual[item] = twice

        sending = jnp.where(
            early,
            jnp.logical_or(turn < 3, leading),
            jnp.where(
                coarse,
                jnp.logical_or(turn < 7, window < windows - 1),
                turn < 9,
            ),
        )
        out_slot = jnp.where(
            early,
            jnp.where(last_early, CHAIN + 1, item),
            jnp.where(
                coarse,
                jnp.where(turn == 7, CHAIN, turn + 1),
                jnp.where(fine, turn - 4, item),
            ),
        )
        out_parity = jnp.where(jnp.logical_or(middle, last_early), 0, (turn + 1) % 2)
        leaving = jnp.logical_and(coarse, turn == 7)
        target = jnp.where(leaving, window + 1, window)

        @pl.when(sending)
        def _():
            source[out_parity, out_slot, 0] = twice[:, 0:LANES]
            source[out_parity, out_slot, 1] = twice[:, LANES:]
            send_state(out_parity, out_slot, target)

            @pl.when(leaving)
            def _():
                for part in range(2):
                    pass_copy(part, target).start()

        out_index = jnp.where(
            early,
            turn,
            jnp.where(
                coarse,
                COARSEN * (turn - 4) + COARSEN - 1,
                jnp.where(fine, COARSEN * (turn - 4), COARSEN * item + turn - 7),
            ),
        )

        @pl.when(jnp.logical_or(jnp.logical_not(early), leading))
        def _():
            out[out_index] = twice[0:width, 0:LANES]

        @pl.when(jnp.logical_and(fresh, jnp.logical_not(handed)))
        def _():
            await_sent(parity, slot)

    def round_of(turn, carry):
        early = turn < 4
        middle = jnp.logical_and(turn >= 4, turn < 8)
        begin = jnp.where(jnp.logical_and(turn >= 8, window == 0), 1, 0)
        jobs = jnp.where(
            middle, jnp.where(jnp.logical_and(turn == 4, window == 0), 0, 2), 4
        )

        def one(item, inner):
            job(turn, item)

            @pl.when(jnp.logical_and(turn < 3, item == 0))
            def _():
                send_drive(turn + 1)

            @pl.when(
                jnp.logical_and(
                    jnp.logical_and(turn == GATED, item == 3), window % 2 == 0
                )
            )
            def _():
                pl.semaphore_signal(
                    gate,
                    inc=1,
                    device_id={"tm": window + 1, "space": place},
                    device_id_type=MESH,
                )

            return inner

        lax.fori_loop(begin, jobs, one, 0)
        return carry

    lax.fori_loop(0, 10, round_of, 0)

    @pl.when(window < windows - 1)
    def _():
        await_sent(0, CHAIN)
        for part in range(2):
            pass_copy(part, window + 1).wait_send()


def shards(initial, forcing, damping, block_inv, coarse_inv, coupling, etype, send_index, conn):
    width = initial.shape[0]
    steps = forcing.shape[0]
    spaces = lax.axis_size("space")
    windows = lax.axis_size("tm")
    vmem = pl.BlockSpec(memory_space=pltpu.VMEM)
    far = pl.BlockSpec(memory_space=pl.ANY)
    dma = pltpu.SemaphoreType.DMA
    return pl.pallas_call(
        functools.partial(kernel, spaces, windows),
        out_shape=jax.ShapeDtypeStruct((steps, width, LANES), BF),
        in_specs=[far, far, vmem, far, far, vmem, vmem, vmem],
        out_specs=vmem,
        scratch_shapes=[
            pltpu.VMEM((width, LANES), BF),
            pltpu.VMEM((steps, width, LANES), BF),
            pltpu.VMEM((4, width, width), BF),
            pltpu.VMEM((FACES, width, width), BF),
            pltpu.VMEM((FACES + 4, ROWS, ROWS), BF),
            pltpu.VMEM((ROWS, DEPTH), BF),
            pltpu.VMEM((16, LANES), F32),
            pltpu.VMEM((2, 8, 2, ROWS, LANES), BF),
            pltpu.VMEM((2, 8, 4, ROWS, LANES), BF),
            pltpu.VMEM((4 * LANES, 13 * LANES), BF),
            pltpu.VMEM((2 * LANES, 12 * LANES), BF),
            pltpu.VMEM((LANES, LANES), BF),
            pltpu.VMEM((4, ROWS, DEPTH), BF),
            pltpu.VMEM((2, ROWS, DEPTH), BF),
            pltpu.VMEM((DEPTH, 2 * LANES), BF),
            pltpu.VMEM((2, ROWS, LANES), BF),
            pltpu.VMEM((2, 8, LANES), F32),
            pltpu.VMEM((4, 4, ROWS, LANES), BF),
            pltpu.VMEM((4, 4, ROWS, LANES), BF),
            pltpu.VMEM((2, 4, 2, ROWS, LANES), BF),
            pltpu.VMEM((4, 2, ROWS, LANES), BF),
            pltpu.VMEM((4, 2, ROWS, LANES), BF),
            pltpu.VMEM((5, ROWS, 2 * LANES), BF),
            pltpu.VMEM((16, LANES), F32),
            pltpu.VMEM((16, LANES), F32),
            dma((4,)),
            dma((2, 8, 4)),
            dma((2, 8, 4)),
            dma((2,)),
            dma((2,)),
            dma((2,)),
            dma((2,)),
            dma((4, 2)),
            dma((4, 2)),
            pltpu.SemaphoreType.REGULAR,
        ],
        compiler_params=pltpu.CompilerParams(
            collective_id=0, has_side_effects=True, vmem_limit_bytes=48 << 20
        ),
    )(
        initial,
        forcing,
        damping[None],
        jnp.concatenate([block_inv, coarse_inv], axis=0),
        coupling,
        etype[None],
        send_index[None],
        conn,
    )


def solution(mesh):
    in_specs = (
        P(None, "space"),
        P("tm", None, "space"),
        P("space"),
        P(),
        P(),
        P(),
        P("space"),
        P("space"),
        P(None, "space"),
    )
    out_specs = P("tm", None, "space")
    return jax.shard_map(shards, mesh=mesh, in_specs=in_specs, out_specs=out_specs, check_vma=False)
```

```python
import functools

import jax
import jax.numpy as jnp
from jax import lax
from jax.experimental import pallas as pl
from jax.experimental.pallas import tpu as pltpu
from jax.sharding import PartitionSpec as P

PRISM = 90
COARSEN = 4
LANES = 128
HALF = 64
ROWS = 144
FACES = 6
DEPTH = (FACES + 1) * ROWS
CHAIN = 4
GATED = 1
HELD = 3
OFFSETS = (1, -1, 2, -2)
MESH = pl.DeviceIdType.MESH
BF = jnp.bfloat16
F32 = jnp.float32


def matmul(left, right):
    return jnp.dot(left, right, preferred_element_type=F32)


def take(table, index):
    return jnp.take_along_axis(table, index, axis=1, mode="promise_in_bounds")


def kernel(
    spaces,
    windows,
    initial_in,
    forcing_in,
    damping,
    inverse_in,
    coupling_in,
    etype,
    send_index,
    conn,
    out,
    initial,
    forcing,
    inverse,
    coupling,
    padded,
    faces,
    meta,
    source,
    received,
    gather_one,
    gather_two,
    pick,
    mats,
    own_mats,
    stacked,
    waiting,
    decay,
    drive,
    drive_sel,
    drive_out,
    drive_left,
    drive_right,
    residual,
    meta_left,
    meta_right,
    load_sem,
    send_sem,
    recv_sem,
    pass_send,
    pass_recv,
    meta_send,
    meta_recv,
    drive_send,
    drive_recv,
    gate,
):
    place = lax.axis_index("space")
    window = lax.axis_index("tm")
    width = initial.shape[0]

    def inside(shift):
        return jnp.logical_and(place + shift >= 0, place + shift < spaces)

    loads = [
        pltpu.make_async_copy(initial_in, initial, load_sem.at[0]),
        pltpu.make_async_copy(forcing_in, forcing, load_sem.at[1]),
        pltpu.make_async_copy(inverse_in, inverse, load_sem.at[2]),
        pltpu.make_async_copy(coupling_in, coupling, load_sem.at[3]),
    ]
    for load in loads:
        load.start()

    received[0, 0:CHAIN] = jnp.zeros((CHAIN,) + received.shape[2:], BF)

    @pl.when(jnp.logical_or(place < 2, place >= spaces - 2))
    def _():
        received[0, CHAIN:] = jnp.zeros((CHAIN,) + received.shape[2:], BF)
        received[1, 0:CHAIN] = jnp.zeros((CHAIN,) + received.shape[2:], BF)
        drive_left[...] = jnp.zeros(drive_left.shape, BF)
        drive_right[...] = jnp.zeros(drive_right.shape, BF)
        meta_left[...] = jnp.zeros(meta_left.shape, F32)
        meta_right[...] = jnp.zeros(meta_right.shape, F32)

    barrier = pltpu.get_barrier_semaphore()
    for shift in OFFSETS:
        @pl.when(inside(shift))
        def _():
            pl.semaphore_signal(
                barrier,
                inc=1,
                device_id={"tm": window, "space": place + shift},
                device_id_type=MESH,
            )
    for shift in (0,) + OFFSETS:
        @pl.when(jnp.logical_and(inside(shift), window > 0))
        def _():
            pl.semaphore_signal(
                barrier,
                inc=1,
                device_id={"tm": window - 1, "space": place + shift},
                device_id_type=MESH,
            )

    def meta_copy(side):
        shift = (1, -1)[side]
        return pltpu.make_async_remote_copy(
            src_ref=meta,
            dst_ref=(meta_left, meta_right)[side],
            send_sem=meta_send.at[side],
            recv_sem=meta_recv.at[side],
            device_id={"tm": window, "space": place + shift},
            device_id_type=MESH,
        )

    def drive_copy(step, side):
        shift = (1, -1)[side]
        return pltpu.make_async_remote_copy(
            src_ref=drive_out.at[side, step],
            dst_ref=(drive_left, drive_right)[side].at[step],
            send_sem=drive_send.at[step, side],
            recv_sem=drive_recv.at[step, side],
            device_id={"tm": window, "space": place + shift},
            device_id_type=MESH,
        )

    def state_copy(parity, slot, direction, target):
        return pltpu.make_async_remote_copy(
            src_ref=source.at[parity, slot, direction // 2],
            dst_ref=received.at[parity, slot, direction],
            send_sem=send_sem.at[parity, slot, direction],
            recv_sem=recv_sem.at[parity, slot, direction],
            device_id={"tm": target, "space": place + OFFSETS[direction]},
            device_id_type=MESH,
        )

    def pass_copy(part, target):
        return pltpu.make_async_remote_copy(
            src_ref=source.at[0, CHAIN, part],
            dst_ref=source.at[0, CHAIN, part],
            send_sem=pass_send.at[part],
            recv_sem=pass_recv.at[part],
            device_id={"tm": target, "space": place},
            device_id_type=MESH,
        )

    def send_state(parity, slot, target):
        for direction in range(4):
            @pl.when(inside(OFFSETS[direction]))
            def _():
                state_copy(parity, slot, direction, target).start()

    def await_state(parity, slot):
        for direction in range(4):
            @pl.when(inside(-OFFSETS[direction]))
            def _():
                state_copy(parity, slot, direction, window).wait_recv()

    def await_sent(parity, slot):
        for direction in range(4):
            @pl.when(inside(OFFSETS[direction]))
            def _():
                state_copy(parity, slot, direction, window).wait_send()

    def send_drive(step):
        for side in range(2):
            @pl.when(inside((1, -1)[side]))
            def _():
                drive_copy(step, side).start()

    def turned(row):
        return jnp.concatenate([row[:, HALF:], row[:, :HALF]], axis=1)

    def fill(step):
        def one(item, carry):
            drive[step, item, 0:width, :] = forcing[item * COARSEN + step]
            drive_sel[step, item] = matmul(drive[step, item], pick[...]).astype(BF)
            return carry

        lax.fori_loop(0, CHAIN, one, 0)
        for pair in range(2):
            even = drive_sel[step, 2 * pair]
            odd = turned(drive_sel[step, 2 * pair + 1])
            drive_out[0, step, pair] = jnp.where(low, odd, even)
            drive_out[1, step, pair] = jnp.where(low, even, odd)

    lane = lax.broadcasted_iota(jnp.int32, (1, LANES), 1)
    low = lane < HALF
    code = lax.broadcasted_iota(jnp.int32, (2 * LANES, LANES), 0)
    spot = lax.broadcasted_iota(jnp.int32, (4 * LANES, LANES), 0)

    meta[...] = jnp.zeros(meta.shape, F32)
    meta[0:1, :] = send_index[...].astype(F32)
    meta[1:2, :] = damping[...]
    meta[2:3, :] = jnp.broadcast_to(etype[...].astype(F32), (1, LANES))
    meta[8 : 8 + FACES, :] = conn[...].astype(F32)
    send_own = send_index[...]
    kind_own = meta[2:3, :]
    pick[...] = (code[0:LANES] == send_own).astype(F32).astype(BF)

    source[0, 0:CHAIN] = jnp.zeros((CHAIN,) + source.shape[2:], BF)
    tall = lax.broadcasted_iota(jnp.int32, (width, LANES), 0)
    kept = jnp.logical_and(
        jnp.logical_or(tall < PRISM, kind_own < 0.5), jnp.broadcast_to(window, (1, 1)) == 0
    )
    loads[0].wait()
    source[0, 0, 0, 0:width, :] = jnp.where(kept, initial[...], jnp.zeros_like(initial))
    source[0, 0, 1] = matmul(source[0, 0, 0], pick[...]).astype(BF)
    drive[:, :, LANES:, :] = jnp.zeros((CHAIN, CHAIN, ROWS - LANES, LANES), BF)
    loads[1].wait()
    fill(0)

    beside_count = sum(jnp.where(inside(shift), 1, 0) for shift in OFFSETS)
    pl.semaphore_wait(
        barrier, beside_count + jnp.where(window < windows - 1, beside_count + 1, 0)
    )
    for side in range(2):
        @pl.when(inside((1, -1)[side]))
        def _():
            meta_copy(side).start()

    @pl.when(window == 0)
    def _():
        send_state(0, 0, window)

    @pl.when(window % 2 == 0)
    def _():
        send_drive(0)

    for load in loads[2:]:
        load.wait()
    padded[...] = jnp.zeros(padded.shape, BF)
    padded[0:FACES, 0:width, 0:width] = -coupling[...]
    padded[FACES:, 0:width, 0:width] = inverse[...]
    across = lax.broadcasted_iota(jnp.int32, (ROWS, DEPTH), 1)
    down = lax.broadcasted_iota(jnp.int32, (ROWS, DEPTH), 0)
    placed = jnp.where(across == down + FACES * ROWS, 1.0, 0.0)
    for face in range(FACES):
        shifted = jnp.where(across == down + face * ROWS, 1.0, 0.0).astype(BF)
        placed = placed + matmul(padded[face], shifted)
    faces[...] = placed.astype(BF)
    for index in range(4):
        mats[index] = matmul(padded[FACES + index], faces[...]).astype(BF)
    for step in range(2):
        own_mats[step] = jnp.where(meta[2:3, 0:1] < 0.5, mats[2 * step], mats[2 * step + 1])

    def spread(row):
        return jnp.broadcast_to(row, (8, LANES))

    def whole(rows):
        return (rows + 0.5).astype(jnp.int32)

    def onehot(rows, index):
        return (rows == index).astype(F32).astype(BF)

    def located(codes, start, listed_at):
        past = jnp.maximum(codes - LANES, 0)
        return jnp.where(codes < LANES, start + codes, take(spread(listed_at), past))

    def second(codes):
        return jnp.where(
            codes < LANES, codes, jnp.where(codes < LANES + HALF, codes + HALF, codes - HALF)
        )

    last_face = lax.broadcasted_iota(jnp.int32, (8, LANES), 0) == FACES - 1

    def masked(index, kind):
        return jnp.where(jnp.logical_and(last_face, kind > 0.5), -1, index)

    conn_own = whole(meta[8:16, :])
    damp_listed = take(meta[0:8, :], spread(send_own))[1:2, :]
    two_own = masked(second(conn_own), kind_own)
    two_listed = masked(second(take(conn_own, spread(send_own))), kind_own)
    for face in range(FACES):
        here = slice(face * LANES, (face + 1) * LANES)
        after = slice((FACES + face) * LANES, (FACES + face + 1) * LANES)
        gather_two[:, here] = onehot(code, two_own[face : face + 1, :])
        gather_two[:, after] = onehot(code, two_listed[face : face + 1, :])

    for step in range(1, 4):
        fill(step)

    for side in range(2):
        @pl.when(inside((-1, 1)[side]))
        def _():
            meta_copy(side).wait_recv()
    for side in range(2):
        @pl.when(inside((1, -1)[side]))
        def _():
            meta_copy(side).wait_send()

    send_left = whole(meta_left[0:1, :])
    send_right = whole(meta_right[0:1, :])
    conn_left = whole(take(meta_left[8:16, :], spread(send_left)))
    conn_right = whole(take(meta_right[8:16, :], spread(send_right)))
    damp_left = take(meta_left[0:8, :], spread(send_left))[1:2, :]
    damp_right = take(meta_right[0:8, :], spread(send_right))[1:2, :]
    damp_beside = jnp.where(low, damp_right, damp_left)
    kind_beside = jnp.where(low, meta_right[2:3, :], meta_left[2:3, :])
    there = jnp.where(
        low,
        jnp.broadcast_to(inside(1).astype(jnp.int32), (1, LANES)),
        jnp.broadcast_to(inside(-1).astype(jnp.int32), (1, LANES)),
    )
    for step in range(2):
        scale = -1.0 if step == 0 else -1.0 * COARSEN
        decay[step, 0:1, :] = jnp.exp(scale * meta[1:2, :])
        decay[step, 1:2, :] = jnp.exp(scale * damp_beside) * there.astype(F32)
        decay[step, 2:3, :] = jnp.exp(scale * damp_listed)
    decay[0, 3:4, :] = kind_own
    decay[0, 4:5, :] = kind_beside

    at_own = located(
        conn_own, LANES, jnp.where(low, turned(send_left), 2 * LANES + turned(send_right))
    )
    at_left = located(
        conn_left, 0, jnp.where(low, 3 * LANES + HALF + lane, LANES + turned(send_own))
    )
    at_right = located(
        conn_right,
        2 * LANES,
        jnp.where(low, LANES + turned(send_own), 3 * LANES + lane - HALF),
    )
    at_own = masked(at_own, kind_own)
    at_beside = masked(jnp.where(low, at_right, at_left), kind_beside)
    at_beside = jnp.where(there > 0, at_beside, -1)
    for face in range(FACES):
        here = slice(face * LANES, (face + 1) * LANES)
        after = slice((FACES + face) * LANES, (FACES + face + 1) * LANES)
        gather_one[:, here] = onehot(spot, at_own[face : face + 1, :])
        gather_one[:, after] = onehot(spot, at_beside[face : face + 1, :])
    at_listed = jnp.where(low, 2 * LANES + send_right, send_left)
    at_listed = jnp.where(there > 0, at_listed, -1)
    gather_one[:, 2 * FACES * LANES :] = onehot(spot, at_listed)

    residual[CHAIN] = jnp.zeros((ROWS, 2 * LANES), BF)

    @pl.when(window % 2 == 1)
    def _():
        pl.semaphore_wait(gate, 1)
        send_drive(0)


    def held(part_now):
        return jnp.where(jnp.logical_and(part_now > 1, window < windows - 1), HELD, 0)

    def job(turn, order):
        early = turn < 4
        ending = jnp.logical_and(turn == 7, window == windows - 1)
        swapped = jnp.where(ending, jnp.where(order < 2, 1 - order, order), order)
        part_now = jnp.where(early, 0, swapped)
        coarse = jnp.logical_and(jnp.logical_not(early), part_now == 0)
        fine = part_now > 0
        shared = jnp.logical_or(coarse, part_now == 1)
        item = jnp.where(
            early, order, jnp.where(coarse, turn - 4, turn - 3 - part_now - held(part_now))
        )
        first = window == 0
        parity = jnp.where(early, turn % 2, jnp.where(part_now == 3, 1, 0))
        slot = jnp.where(shared, turn, item)
        op = jnp.where(coarse, 1, 0)

        fresh = jnp.where(
            early,
            jnp.logical_or(turn >= 1, jnp.logical_and(item == 0, first)),
            jnp.logical_or(jnp.logical_not(shared), order == 0),
        )
        handed = jnp.logical_and(turn == 4, order == 0)

        @pl.when(handed)
        def _():
            for part in range(2):
                pass_copy(part, window).wait_recv()

        @pl.when(jnp.logical_and(early, item == 0))
        def _():
            for side in range(2):
                @pl.when(inside((-1, 1)[side]))
                def _():
                    drive_copy(turn, side).wait_recv()
            for side in range(2):
                @pl.when(inside((1, -1)[side]))
                def _():
                    drive_copy(turn, side).wait_send()

        fine_step = jnp.where(early, turn, jnp.where(coarse, 0, part_now - 1))
        fine_item = item
        drive_at = jnp.where(coarse, 0.0, 1.0)

        own = source[parity, slot, 0]
        listed = source[parity, slot, 1]
        decay_now = decay[op]
        from_left = drive_left[fine_step, fine_item // 2]
        from_right = drive_right[fine_step, fine_item // 2]
        drive_beside = jnp.where(
            jnp.broadcast_to(fine_item % 2, (1, 1)) == 0,
            jnp.where(low, from_right, from_left),
            turned(jnp.where(low, from_left, from_right)),
        )
        rhs_own = decay_now[0:1, :] * own.astype(F32) + drive_at * drive[
            fine_step, fine_item
        ].astype(F32)
        rhs_listed = decay_now[2:3, :] * listed.astype(F32) + drive_at * drive_sel[
            fine_step, fine_item
        ].astype(F32)

        def stack(gathered):
            gathered = gathered.astype(BF)
            for face in range(FACES):
                rows = slice(face * ROWS, (face + 1) * ROWS)
                stacked[rows, 0:LANES] = gathered[:, face * LANES : (face + 1) * LANES]
                stacked[rows, LANES : 2 * LANES] = gathered[
                    :, (FACES + face) * LANES : (FACES + face + 1) * LANES
                ]

        tail = slice(FACES * ROWS, DEPTH)
        stacked[tail, 0:LANES] = rhs_own.astype(BF)
        waiting[0] = rhs_listed.astype(BF)
        waiting[1] = (drive_at * drive_beside.astype(F32)).astype(BF)

        @pl.when(fresh)
        def _():
            await_state(parity, slot)

        outer = jnp.where(low, received[parity, slot, 3], received[parity, slot, 2])
        near = jnp.concatenate([received[parity, slot, 0], own], axis=1)
        far = jnp.concatenate([received[parity, slot, 1], outer], axis=1)
        gathered = matmul(near, gather_one[0 : 2 * LANES, :]) + matmul(
            far, gather_one[2 * LANES :, :]
        )
        stack(gathered)
        rhs_beside = decay_now[1:2, :] * gathered[
            :, 2 * FACES * LANES :
        ] + waiting[1].astype(F32)
        stacked[tail, LANES : 2 * LANES] = rhs_beside.astype(BF)
        kinds = jnp.concatenate([decay[0, 3:4, :], decay[0, 4:5, :]], axis=1)
        once = jnp.where(
            kinds < 0.5,
            matmul(mats[2 * op], stacked[...]),
            matmul(mats[2 * op + 1], stacked[...]),
        ).astype(BF)

        stack(matmul(once, gather_two[...]))
        stacked[tail, LANES : 2 * LANES] = waiting[0]
        plus = residual[jnp.where(coarse, item, CHAIN)].astype(F32)
        twice = (matmul(own_mats[op], stacked[...]) + plus).astype(BF)

        leading = jnp.logical_and(first, item == 0)
        last_early = turn == 3

        @pl.when(last_early)
        def _():
            residual[item] = twice

        sending = jnp.where(
            early,
            jnp.logical_or(turn < 3, leading),
            jnp.where(coarse, jnp.logical_or(turn < 7, window < windows - 1), part_now < 3),
        )
        out_slot = jnp.where(
            early,
            jnp.where(last_early, CHAIN + 1, item),
            jnp.where(coarse, jnp.where(turn == 7, CHAIN, turn + 1), item),
        )
        out_parity = jnp.where(
            early,
            jnp.where(last_early, 0, (turn + 1) % 2),
            jnp.where(part_now == 2, 1, 0),
        )
        leaving = jnp.logical_and(coarse, turn == 7)
        target = jnp.where(leaving, window + 1, window)

        @pl.when(sending)
        def _():
            source[out_parity, out_slot, 0] = twice[:, 0:LANES]
            source[out_parity, out_slot, 1] = twice[:, LANES:]
            send_state(out_parity, out_slot, target)

            @pl.when(leaving)
            def _():
                for part in range(2):
                    pass_copy(part, target).start()

        out_index = jnp.where(
            early,
            turn,
            COARSEN * item + jnp.where(coarse, COARSEN - 1, part_now - 1),
        )

        @pl.when(jnp.logical_or(jnp.logical_not(early), leading))
        def _():
            out[out_index] = twice[0:width, 0:LANES]

        @pl.when(jnp.logical_and(fresh, jnp.logical_not(handed)))
        def _():
            await_sent(parity, slot)

    def round_of(turn, carry):
        early = turn < 4
        begin = jnp.where(turn >= 8, 2, 0)

        def one(item, inner):
            interval = turn - 3 - item - held(item)
            counted = jnp.logical_and(
                jnp.logical_and(interval >= 0, interval <= 3),
                jnp.logical_or(window > 0, interval > 0),
            )
            stepped = jnp.where(
                item == 0,
                jnp.logical_or(window > 0, turn > 4),
                counted,
            )

            @pl.when(jnp.logical_or(early, stepped))
            def _():
                job(turn, item)

            @pl.when(jnp.logical_and(turn < 3, item == 0))
            def _():
                send_drive(turn + 1)

            @pl.when(
                jnp.logical_and(
                    jnp.logical_and(turn == GATED, item == 3), window % 2 == 0
                )
            )
            def _():
                pl.semaphore_signal(
                    gate,
                    inc=1,
                    device_id={"tm": window + 1, "space": place},
                    device_id_type=MESH,
                )

            return inner

        lax.fori_loop(begin, 4, one, 0)
        return carry

    lax.fori_loop(0, jnp.where(window < windows - 1, 10 + HELD, 10), round_of, 0)

    @pl.when(window < windows - 1)
    def _():
        await_sent(0, CHAIN)
        for part in range(2):
            pass_copy(part, window + 1).wait_send()


def shards(initial, forcing, damping, block_inv, coarse_inv, coupling, etype, send_index, conn):
    width = initial.shape[0]
    steps = forcing.shape[0]
    spaces = lax.axis_size("space")
    windows = lax.axis_size("tm")
    vmem = pl.BlockSpec(memory_space=pltpu.VMEM)
    far = pl.BlockSpec(memory_space=pl.ANY)
    dma = pltpu.SemaphoreType.DMA
    return pl.pallas_call(
        functools.partial(kernel, spaces, windows),
        out_shape=jax.ShapeDtypeStruct((steps, width, LANES), BF),
        in_specs=[far, far, vmem, far, far, vmem, vmem, vmem],
        out_specs=vmem,
        scratch_shapes=[
            pltpu.VMEM((width, LANES), BF),
            pltpu.VMEM((steps, width, LANES), BF),
            pltpu.VMEM((4, width, width), BF),
            pltpu.VMEM((FACES, width, width), BF),
            pltpu.VMEM((FACES + 4, ROWS, ROWS), BF),
            pltpu.VMEM((ROWS, DEPTH), BF),
            pltpu.VMEM((16, LANES), F32),
            pltpu.VMEM((2, 8, 2, ROWS, LANES), BF),
            pltpu.VMEM((2, 8, 4, ROWS, LANES), BF),
            pltpu.VMEM((4 * LANES, 13 * LANES), BF),
            pltpu.VMEM((2 * LANES, 12 * LANES), BF),
            pltpu.VMEM((LANES, LANES), BF),
            pltpu.VMEM((4, ROWS, DEPTH), BF),
            pltpu.VMEM((2, ROWS, DEPTH), BF),
            pltpu.VMEM((DEPTH, 2 * LANES), BF),
            pltpu.VMEM((2, ROWS, LANES), BF),
            pltpu.VMEM((2, 8, LANES), F32),
            pltpu.VMEM((4, 4, ROWS, LANES), BF),
            pltpu.VMEM((4, 4, ROWS, LANES), BF),
            pltpu.VMEM((2, 4, 2, ROWS, LANES), BF),
            pltpu.VMEM((4, 2, ROWS, LANES), BF),
            pltpu.VMEM((4, 2, ROWS, LANES), BF),
            pltpu.VMEM((5, ROWS, 2 * LANES), BF),
            pltpu.VMEM((16, LANES), F32),
            pltpu.VMEM((16, LANES), F32),
            dma((4,)),
            dma((2, 8, 4)),
            dma((2, 8, 4)),
            dma((2,)),
            dma((2,)),
            dma((2,)),
            dma((2,)),
            dma((4, 2)),
            dma((4, 2)),
            pltpu.SemaphoreType.REGULAR,
        ],
        compiler_params=pltpu.CompilerParams(
            collective_id=0, has_side_effects=True, vmem_limit_bytes=48 << 20
        ),
    )(
        initial,
        forcing,
        damping[None],
        jnp.concatenate([block_inv, coarse_inv], axis=0),
        coupling,
        etype[None],
        send_index[None],
        conn,
    )


def solution(mesh):
    in_specs = (
        P(None, "space"),
        P("tm", None, "space"),
        P("space"),
        P(),
        P(),
        P(),
        P("space"),
        P("space"),
        P(None, "space"),
    )
    out_specs = P("tm", None, "space")
    return jax.shard_map(shards, mesh=mesh, in_specs=in_specs, out_specs=out_specs, check_vma=False)
```

```python
import functools

import jax
import jax.numpy as jnp
from jax import lax
from jax.experimental import pallas as pl
from jax.experimental.pallas import tpu as pltpu
from jax.sharding import PartitionSpec as P

PRISM = 90
COARSEN = 4
LANES = 128
HALF = 64
ROWS = 144
FACES = 6
DEPTH = (FACES + 1) * ROWS
CHAIN = 4
GATED = 1
HELD = 3
OFFSETS = (1, -1, 2, -2)
MESH = pl.DeviceIdType.MESH
BF = jnp.bfloat16
F32 = jnp.float32


def matmul(left, right):
    return jnp.dot(left, right, preferred_element_type=F32)


def take(table, index):
    return jnp.take_along_axis(table, index, axis=1, mode="promise_in_bounds")


def kernel(
    spaces,
    windows,
    initial_in,
    forcing_in,
    damping,
    inverse_in,
    coupling_in,
    etype,
    send_index,
    conn,
    out,
    initial,
    forcing,
    inverse,
    coupling,
    padded,
    faces,
    meta,
    source,
    received,
    gather_one,
    gather_two,
    pick,
    mats,
    own_mats,
    stacked,
    waiting,
    decay,
    drive,
    drive_sel,
    drive_out,
    drive_left,
    drive_right,
    residual,
    meta_left,
    meta_right,
    load_sem,
    send_sem,
    recv_sem,
    pass_send,
    pass_recv,
    meta_send,
    meta_recv,
    drive_send,
    drive_recv,
    gate,
):
    place = lax.axis_index("space")
    window = lax.axis_index("tm")
    width = initial.shape[0]

    def inside(shift):
        return jnp.logical_and(place + shift >= 0, place + shift < spaces)

    loads = [
        pltpu.make_async_copy(initial_in, initial, load_sem.at[0]),
        pltpu.make_async_copy(forcing_in, forcing, load_sem.at[1]),
        pltpu.make_async_copy(inverse_in, inverse, load_sem.at[2]),
        pltpu.make_async_copy(coupling_in, coupling, load_sem.at[3]),
    ]
    for load in loads:
        load.start()

    received[0, 0:CHAIN] = jnp.zeros((CHAIN,) + received.shape[2:], BF)

    @pl.when(jnp.logical_or(place < 2, place >= spaces - 2))
    def _():
        received[0, CHAIN:] = jnp.zeros((CHAIN,) + received.shape[2:], BF)
        received[1, 0:CHAIN] = jnp.zeros((CHAIN,) + received.shape[2:], BF)
        drive_left[...] = jnp.zeros(drive_left.shape, BF)
        drive_right[...] = jnp.zeros(drive_right.shape, BF)
        meta_left[...] = jnp.zeros(meta_left.shape, F32)
        meta_right[...] = jnp.zeros(meta_right.shape, F32)

    barrier = pltpu.get_barrier_semaphore()
    for shift in OFFSETS:
        @pl.when(inside(shift))
        def _():
            pl.semaphore_signal(
                barrier,
                inc=1,
                device_id={"tm": window, "space": place + shift},
                device_id_type=MESH,
            )
    for shift in (0,) + OFFSETS:
        @pl.when(jnp.logical_and(inside(shift), window > 0))
        def _():
            pl.semaphore_signal(
                barrier,
                inc=1,
                device_id={"tm": window - 1, "space": place + shift},
                device_id_type=MESH,
            )

    def meta_copy(side):
        shift = (1, -1)[side]
        return pltpu.make_async_remote_copy(
            src_ref=meta,
            dst_ref=(meta_left, meta_right)[side],
            send_sem=meta_send.at[side],
            recv_sem=meta_recv.at[side],
            device_id={"tm": window, "space": place + shift},
            device_id_type=MESH,
        )

    def drive_copy(step, side):
        shift = (1, -1)[side]
        return pltpu.make_async_remote_copy(
            src_ref=drive_out.at[side, step],
            dst_ref=(drive_left, drive_right)[side].at[step],
            send_sem=drive_send.at[step, side],
            recv_sem=drive_recv.at[step, side],
            device_id={"tm": window, "space": place + shift},
            device_id_type=MESH,
        )

    def state_copy(parity, slot, direction, target):
        return pltpu.make_async_remote_copy(
            src_ref=source.at[parity, slot, direction // 2],
            dst_ref=received.at[parity, slot, direction],
            send_sem=send_sem.at[parity, slot, direction],
            recv_sem=recv_sem.at[parity, slot, direction],
            device_id={"tm": target, "space": place + OFFSETS[direction]},
            device_id_type=MESH,
        )

    def pass_copy(part, target):
        return pltpu.make_async_remote_copy(
            src_ref=source.at[0, CHAIN, part],
            dst_ref=source.at[0, CHAIN, part],
            send_sem=pass_send.at[part],
            recv_sem=pass_recv.at[part],
            device_id={"tm": target, "space": place},
            device_id_type=MESH,
        )

    def send_state(parity, slot, target):
        for direction in range(4):
            @pl.when(inside(OFFSETS[direction]))
            def _():
                state_copy(parity, slot, direction, target).start()

    def await_state(parity, slot):
        for direction in range(4):
            @pl.when(inside(-OFFSETS[direction]))
            def _():
                state_copy(parity, slot, direction, window).wait_recv()

    def await_sent(parity, slot):
        for direction in range(4):
            @pl.when(inside(OFFSETS[direction]))
            def _():
                state_copy(parity, slot, direction, window).wait_send()

    def send_drive(step):
        for side in range(2):
            @pl.when(inside((1, -1)[side]))
            def _():
                drive_copy(step, side).start()

    def turned(row):
        return jnp.concatenate([row[:, HALF:], row[:, :HALF]], axis=1)

    def fill(step):
        def one(item, carry):
            drive[step, item, 0:width, :] = forcing[item * COARSEN + step]
            drive_sel[step, item] = matmul(drive[step, item], pick[...]).astype(BF)
            return carry

        lax.fori_loop(0, CHAIN, one, 0)
        for pair in range(2):
            even = drive_sel[step, 2 * pair]
            odd = turned(drive_sel[step, 2 * pair + 1])
            drive_out[0, step, pair] = jnp.where(low, odd, even)
            drive_out[1, step, pair] = jnp.where(low, even, odd)

    lane = lax.broadcasted_iota(jnp.int32, (1, LANES), 1)
    low = lane < HALF
    code = lax.broadcasted_iota(jnp.int32, (2 * LANES, LANES), 0)
    spot = lax.broadcasted_iota(jnp.int32, (4 * LANES, LANES), 0)

    meta[...] = jnp.zeros(meta.shape, F32)
    meta[0:1, :] = send_index[...].astype(F32)
    meta[1:2, :] = damping[...]
    meta[2:3, :] = jnp.broadcast_to(etype[...].astype(F32), (1, LANES))
    meta[8 : 8 + FACES, :] = conn[...].astype(F32)
    send_own = send_index[...]
    kind_own = meta[2:3, :]
    pick[...] = (code[0:LANES] == send_own).astype(F32).astype(BF)

    source[0, 0:CHAIN] = jnp.zeros((CHAIN,) + source.shape[2:], BF)
    tall = lax.broadcasted_iota(jnp.int32, (width, LANES), 0)
    kept = jnp.logical_and(
        jnp.logical_or(tall < PRISM, kind_own < 0.5), jnp.broadcast_to(window, (1, 1)) == 0
    )
    loads[0].wait()
    source[0, 0, 0, 0:width, :] = jnp.where(kept, initial[...], jnp.zeros_like(initial))
    source[0, 0, 1] = matmul(source[0, 0, 0], pick[...]).astype(BF)
    drive[:, :, LANES:, :] = jnp.zeros((CHAIN, CHAIN, ROWS - LANES, LANES), BF)
    loads[1].wait()
    fill(0)

    beside_count = sum(jnp.where(inside(shift), 1, 0) for shift in OFFSETS)
    pl.semaphore_wait(
        barrier, beside_count + jnp.where(window < windows - 1, beside_count + 1, 0)
    )
    for side in range(2):
        @pl.when(inside((1, -1)[side]))
        def _():
            meta_copy(side).start()

    @pl.when(window == 0)
    def _():
        send_state(0, 0, window)

    @pl.when(window % 2 == 0)
    def _():
        send_drive(0)

    for load in loads[2:]:
        load.wait()
    padded[...] = jnp.zeros(padded.shape, BF)
    padded[0:FACES, 0:width, 0:width] = -coupling[...]
    padded[FACES:, 0:width, 0:width] = inverse[...]
    across = lax.broadcasted_iota(jnp.int32, (ROWS, DEPTH), 1)
    down = lax.broadcasted_iota(jnp.int32, (ROWS, DEPTH), 0)
    placed = jnp.where(across == down + FACES * ROWS, 1.0, 0.0)
    for face in range(FACES):
        shifted = jnp.where(across == down + face * ROWS, 1.0, 0.0).astype(BF)
        placed = placed + matmul(padded[face], shifted)
    faces[...] = placed.astype(BF)
    for index in range(4):
        mats[index] = matmul(padded[FACES + index], faces[...]).astype(BF)
    for step in range(2):
        own_mats[step] = jnp.where(meta[2:3, 0:1] < 0.5, mats[2 * step], mats[2 * step + 1])

    def spread(row):
        return jnp.broadcast_to(row, (8, LANES))

    def whole(rows):
        return (rows + 0.5).astype(jnp.int32)

    def onehot(rows, index):
        return (rows == index).astype(F32).astype(BF)

    def located(codes, start, listed_at):
        past = jnp.maximum(codes - LANES, 0)
        return jnp.where(codes < LANES, start + codes, take(spread(listed_at), past))

    def second(codes):
        return jnp.where(
            codes < LANES, codes, jnp.where(codes < LANES + HALF, codes + HALF, codes - HALF)
        )

    last_face = lax.broadcasted_iota(jnp.int32, (8, LANES), 0) == FACES - 1

    def masked(index, kind):
        return jnp.where(jnp.logical_and(last_face, kind > 0.5), -1, index)

    conn_own = whole(meta[8:16, :])
    damp_listed = take(meta[0:8, :], spread(send_own))[1:2, :]
    two_own = masked(second(conn_own), kind_own)
    two_listed = masked(second(take(conn_own, spread(send_own))), kind_own)
    for face in range(FACES):
        here = slice(face * LANES, (face + 1) * LANES)
        after = slice((FACES + face) * LANES, (FACES + face + 1) * LANES)
        gather_two[:, here] = onehot(code, two_own[face : face + 1, :])
        gather_two[:, after] = onehot(code, two_listed[face : face + 1, :])

    for step in range(1, 4):
        fill(step)

    for side in range(2):
        @pl.when(inside((-1, 1)[side]))
        def _():
            meta_copy(side).wait_recv()
    for side in range(2):
        @pl.when(inside((1, -1)[side]))
        def _():
            meta_copy(side).wait_send()

    send_left = whole(meta_left[0:1, :])
    send_right = whole(meta_right[0:1, :])
    conn_left = whole(take(meta_left[8:16, :], spread(send_left)))
    conn_right = whole(take(meta_right[8:16, :], spread(send_right)))
    damp_left = take(meta_left[0:8, :], spread(send_left))[1:2, :]
    damp_right = take(meta_right[0:8, :], spread(send_right))[1:2, :]
    damp_beside = jnp.where(low, damp_right, damp_left)
    kind_beside = jnp.where(low, meta_right[2:3, :], meta_left[2:3, :])
    there = jnp.where(
        low,
        jnp.broadcast_to(inside(1).astype(jnp.int32), (1, LANES)),
        jnp.broadcast_to(inside(-1).astype(jnp.int32), (1, LANES)),
    )
    for step in range(2):
        scale = -1.0 if step == 0 else -1.0 * COARSEN
        decay[step, 0:1, :] = jnp.exp(scale * meta[1:2, :])
        decay[step, 1:2, :] = jnp.exp(scale * damp_beside) * there.astype(F32)
        decay[step, 2:3, :] = jnp.exp(scale * damp_listed)
    decay[0, 3:4, :] = kind_own
    decay[0, 4:5, :] = kind_beside

    at_own = located(
        conn_own, LANES, jnp.where(low, turned(send_left), 2 * LANES + turned(send_right))
    )
    at_left = located(
        conn_left, 0, jnp.where(low, 3 * LANES + HALF + lane, LANES + turned(send_own))
    )
    at_right = located(
        conn_right,
        2 * LANES,
        jnp.where(low, LANES + turned(send_own), 3 * LANES + lane - HALF),
    )
    at_own = masked(at_own, kind_own)
    at_beside = masked(jnp.where(low, at_right, at_left), kind_beside)
    at_beside = jnp.where(there > 0, at_beside, -1)
    for face in range(FACES):
        here = slice(face * LANES, (face + 1) * LANES)
        after = slice((FACES + face) * LANES, (FACES + face + 1) * LANES)
        gather_one[:, here] = onehot(spot, at_own[face : face + 1, :])
        gather_one[:, after] = onehot(spot, at_beside[face : face + 1, :])
    at_listed = jnp.where(low, 2 * LANES + send_right, send_left)
    at_listed = jnp.where(there > 0, at_listed, -1)
    gather_one[:, 2 * FACES * LANES :] = onehot(spot, at_listed)

    residual[CHAIN] = jnp.zeros((ROWS, 2 * LANES), BF)

    @pl.when(window % 2 == 1)
    def _():
        pl.semaphore_wait(gate, 1)
        send_drive(0)


    def held(part_now):
        return jnp.where(jnp.logical_and(part_now > 1, window < windows - 1), HELD, 0)

    def job(turn, order):
        early = turn < 4
        ending = jnp.logical_and(turn == 7, window == windows - 1)
        swapped = jnp.where(ending, jnp.where(order < 2, 1 - order, order), order)
        part_now = jnp.where(early, 0, swapped)
        coarse = jnp.logical_and(jnp.logical_not(early), part_now == 0)
        fine = part_now > 0
        shared = jnp.logical_or(coarse, part_now == 1)
        item = jnp.where(
            early, order, jnp.where(coarse, turn - 4, turn - 3 - part_now - held(part_now))
        )
        first = window == 0
        parity = jnp.where(early, turn % 2, jnp.where(part_now == 3, 1, 0))
        slot = jnp.where(shared, turn, item)
        op = jnp.where(coarse, 1, 0)

        fresh = jnp.where(
            early,
            jnp.logical_or(turn >= 1, jnp.logical_and(item == 0, first)),
            jnp.logical_or(jnp.logical_not(shared), order == 0),
        )
        handed = jnp.logical_and(turn == 4, order == 0)

        @pl.when(handed)
        def _():
            for part in range(2):
                pass_copy(part, window).wait_recv()

        @pl.when(jnp.logical_and(early, item == 0))
        def _():
            for side in range(2):
                @pl.when(inside((-1, 1)[side]))
                def _():
                    drive_copy(turn, side).wait_recv()
            for side in range(2):
                @pl.when(inside((1, -1)[side]))
                def _():
                    drive_copy(turn, side).wait_send()

        fine_step = jnp.where(early, turn, jnp.where(coarse, 0, part_now - 1))
        fine_item = item
        drive_at = jnp.where(coarse, 0.0, 1.0)

        own = source[parity, slot, 0]
        listed = source[parity, slot, 1]
        decay_now = decay[op]
        from_left = drive_left[fine_step, fine_item // 2]
        from_right = drive_right[fine_step, fine_item // 2]
        drive_beside = jnp.where(
            jnp.broadcast_to(fine_item % 2, (1, 1)) == 0,
            jnp.where(low, from_right, from_left),
            turned(jnp.where(low, from_left, from_right)),
        )
        rhs_own = decay_now[0:1, :] * own.astype(F32) + drive_at * drive[
            fine_step, fine_item
        ].astype(F32)
        rhs_listed = decay_now[2:3, :] * listed.astype(F32) + drive_at * drive_sel[
            fine_step, fine_item
        ].astype(F32)

        def stack(gathered):
            gathered = gathered.astype(BF)
            for face in range(FACES):
                rows = slice(face * ROWS, (face + 1) * ROWS)
                stacked[rows, 0:LANES] = gathered[:, face * LANES : (face + 1) * LANES]
                stacked[rows, LANES : 2 * LANES] = gathered[
                    :, (FACES + face) * LANES : (FACES + face + 1) * LANES
                ]

        tail = slice(FACES * ROWS, DEPTH)
        stacked[tail, 0:LANES] = rhs_own.astype(BF)
        waiting[0] = rhs_listed.astype(BF)
        waiting[1] = drive_beside * drive_at.astype(BF)

        @pl.when(fresh)
        def _():
            await_state(parity, slot)

        outer = jnp.where(low, received[parity, slot, 3], received[parity, slot, 2])
        near = jnp.concatenate([received[parity, slot, 0], own], axis=1)
        far = jnp.concatenate([received[parity, slot, 1], outer], axis=1)
        gathered = matmul(near, gather_one[0 : 2 * LANES, :]) + matmul(
            far, gather_one[2 * LANES :, :]
        )
        stack(gathered)
        rhs_beside = decay_now[1:2, :] * gathered[
            :, 2 * FACES * LANES :
        ] + waiting[1].astype(F32)
        stacked[tail, LANES : 2 * LANES] = rhs_beside.astype(BF)
        kinds = jnp.concatenate([decay[0, 3:4, :], decay[0, 4:5, :]], axis=1)
        once = jnp.where(
            kinds < 0.5,
            matmul(mats[2 * op], stacked[...]),
            matmul(mats[2 * op + 1], stacked[...]),
        ).astype(BF)

        stack(matmul(once, gather_two[...]))
        stacked[tail, LANES : 2 * LANES] = waiting[0]
        plus = residual[jnp.where(coarse, item, CHAIN)].astype(F32)
        twice = (matmul(own_mats[op], stacked[...]) + plus).astype(BF)

        leading = jnp.logical_and(first, item == 0)
        last_early = turn == 3

        @pl.when(last_early)
        def _():
            residual[item] = twice

        sending = jnp.where(
            early,
            jnp.logical_or(turn < 3, leading),
            jnp.where(coarse, jnp.logical_or(turn < 7, window < windows - 1), part_now < 3),
        )
        out_slot = jnp.where(
            early,
            jnp.where(last_early, CHAIN + 1, item),
            jnp.where(coarse, jnp.where(turn == 7, CHAIN, turn + 1), item),
        )
        out_parity = jnp.where(
            early,
            jnp.where(last_early, 0, (turn + 1) % 2),
            jnp.where(part_now == 2, 1, 0),
        )
        leaving = jnp.logical_and(coarse, turn == 7)
        target = jnp.where(leaving, window + 1, window)

        @pl.when(sending)
        def _():
            source[out_parity, out_slot, 0] = twice[:, 0:LANES]
            source[out_parity, out_slot, 1] = twice[:, LANES:]
            send_state(out_parity, out_slot, target)

            @pl.when(leaving)
            def _():
                for part in range(2):
                    pass_copy(part, target).start()

        out_index = jnp.where(
            early,
            turn,
            COARSEN * item + jnp.where(coarse, COARSEN - 1, part_now - 1),
        )

        @pl.when(jnp.logical_or(jnp.logical_not(early), leading))
        def _():
            out[out_index] = twice[0:width, 0:LANES]

        @pl.when(jnp.logical_and(fresh, jnp.logical_not(handed)))
        def _():
            await_sent(parity, slot)

    def round_of(turn, carry):
        early = turn < 4
        begin = jnp.where(turn >= 8, 2, 0)

        def one(item, inner):
            interval = turn - 3 - item - held(item)
            counted = jnp.logical_and(
                jnp.logical_and(interval >= 0, interval <= 3),
                jnp.logical_or(window > 0, interval > 0),
            )
            stepped = jnp.where(
                item == 0,
                jnp.logical_or(window > 0, turn > 4),
                counted,
            )

            @pl.when(jnp.logical_or(early, stepped))
            def _():
                job(turn, item)

            @pl.when(jnp.logical_and(turn < 3, item == 0))
            def _():
                send_drive(turn + 1)

            @pl.when(
                jnp.logical_and(
                    jnp.logical_and(turn == GATED, item == 3), window % 2 == 0
                )
            )
            def _():
                pl.semaphore_signal(
                    gate,
                    inc=1,
                    device_id={"tm": window + 1, "space": place},
                    device_id_type=MESH,
                )

            return inner

        lax.fori_loop(begin, 4, one, 0)
        return carry

    lax.fori_loop(0, jnp.where(window < windows - 1, 10 + HELD, 10), round_of, 0)

    @pl.when(window < windows - 1)
    def _():
        await_sent(0, CHAIN)
        for part in range(2):
            pass_copy(part, window + 1).wait_send()


def shards(initial, forcing, damping, block_inv, coarse_inv, coupling, etype, send_index, conn):
    width = initial.shape[0]
    steps = forcing.shape[0]
    spaces = lax.axis_size("space")
    windows = lax.axis_size("tm")
    vmem = pl.BlockSpec(memory_space=pltpu.VMEM)
    far = pl.BlockSpec(memory_space=pl.ANY)
    dma = pltpu.SemaphoreType.DMA
    return pl.pallas_call(
        functools.partial(kernel, spaces, windows),
        out_shape=jax.ShapeDtypeStruct((steps, width, LANES), BF),
        in_specs=[far, far, vmem, far, far, vmem, vmem, vmem],
        out_specs=vmem,
        scratch_shapes=[
            pltpu.VMEM((width, LANES), BF),
            pltpu.VMEM((steps, width, LANES), BF),
            pltpu.VMEM((4, width, width), BF),
            pltpu.VMEM((FACES, width, width), BF),
            pltpu.VMEM((FACES + 4, ROWS, ROWS), BF),
            pltpu.VMEM((ROWS, DEPTH), BF),
            pltpu.VMEM((16, LANES), F32),
            pltpu.VMEM((2, 8, 2, ROWS, LANES), BF),
            pltpu.VMEM((2, 8, 4, ROWS, LANES), BF),
            pltpu.VMEM((4 * LANES, 13 * LANES), BF),
            pltpu.VMEM((2 * LANES, 12 * LANES), BF),
            pltpu.VMEM((LANES, LANES), BF),
            pltpu.VMEM((4, ROWS, DEPTH), BF),
            pltpu.VMEM((2, ROWS, DEPTH), BF),
            pltpu.VMEM((DEPTH, 2 * LANES), BF),
            pltpu.VMEM((2, ROWS, LANES), BF),
            pltpu.VMEM((2, 8, LANES), F32),
            pltpu.VMEM((4, 4, ROWS, LANES), BF),
            pltpu.VMEM((4, 4, ROWS, LANES), BF),
            pltpu.VMEM((2, 4, 2, ROWS, LANES), BF),
            pltpu.VMEM((4, 2, ROWS, LANES), BF),
            pltpu.VMEM((4, 2, ROWS, LANES), BF),
            pltpu.VMEM((5, ROWS, 2 * LANES), BF),
            pltpu.VMEM((16, LANES), F32),
            pltpu.VMEM((16, LANES), F32),
            dma((4,)),
            dma((2, 8, 4)),
            dma((2, 8, 4)),
            dma((2,)),
            dma((2,)),
            dma((2,)),
            dma((2,)),
            dma((4, 2)),
            dma((4, 2)),
            pltpu.SemaphoreType.REGULAR,
        ],
        compiler_params=pltpu.CompilerParams(
            collective_id=0, has_side_effects=True, vmem_limit_bytes=48 << 20
        ),
    )(
        initial,
        forcing,
        damping[None],
        jnp.concatenate([block_inv, coarse_inv], axis=0),
        coupling,
        etype[None],
        send_index[None],
        conn,
    )


def solution(mesh):
    in_specs = (
        P(None, "space"),
        P("tm", None, "space"),
        P("space"),
        P(),
        P(),
        P(),
        P("space"),
        P("space"),
        P(None, "space"),
    )
    out_specs = P("tm", None, "space")
    return jax.shard_map(shards, mesh=mesh, in_specs=in_specs, out_specs=out_specs, check_vma=False)
```
